32 devices in a mesh: rep: 8 (over y, x, core), shard: 4 (over z).
Axes of the slice: x: 2, y: 2, z: 4, core: 2. Of those that a mesh axis runs over, the one named last changes fastest.
Arguments:
- tokens: bfloat16 [8192, 512], P(('rep', 'shard')), may hold values from -6 to 6
- cotangent: bfloat16 [8192, 512], P(('rep', 'shard')), may hold values from -6 to 6
- block_fill: int32 [64], P(('rep', 'shard')), may hold values from 0 to 128, as said below
- block_start: int32 [64], P(('rep', 'shard')), may hold values from 0 to 1, as said below
- in_weight: float32 [512, 2320], P('shard'), may hold values from -0.25 to 0.25
- out_weight: float32 [1024, 512], P('shard'), may hold values from -0.1875 to 0.1875
- in_moment: float32 [512, 2320], P('shard'), may hold values from -1.5 to 1.5
- out_moment: float32 [1024, 512], P('shard'), may hold values from -4 to 4
- norm_gain: float32 [512], replicated, may hold values from 0.5 to 1.5
- gate_gain: float32 [1024], replicated, may hold values from 0.5 to 1.5
- conv_params: float32 [5, 1280], replicated, may hold values from -0.5 to 0.5
- head_params: float32 [3, 16], replicated, may hold values from -6.3 to 1.5
- adam_norm: float32 [2, 512], replicated, may hold values from -0.2 to 0.2, as said below
- adam_gate: float32 [2, 1024], replicated, may hold values from -0.2 to 0.2, as said below
- adam_conv: float32 [2, 5, 1280], replicated, may hold values from -0.2 to 0.2, as said below
- adam_head: float32 [2, 3, 16], replicated, may hold values from -0.2 to 0.2, as said below
Outputs:
- activations: bfloat16 [8192, 512], P(('rep', 'shard'))
- input_grad: float32 [8192, 512], P(('rep', 'shard'))
- grad_in_weight: float32 [512, 2320], P('shard')
- grad_out_weight: float32 [1024, 512], P('shard')
- grad_norm_gain: float32 [512], replicated
- grad_gate_gain: float32 [1024], replicated
- grad_conv: float32 [5, 1280], replicated
- grad_head: float32 [3, 16], replicated
- new_in_weight: float32 [512, 2320], P('shard')
- new_out_weight: float32 [1024, 512], P('shard')
- new_in_moment: float32 [512, 2320], P('shard')
- new_out_moment: float32 [1024, 512], P('shard')
- new_norm_gain: float32 [512], replicated
- new_gate_gain: float32 [1024], replicated
- new_conv_params: float32 [5, 1280], replicated
- new_head_params: float32 [3, 16], replicated
- new_adam_norm: float32 [2, 512], replicated
- new_adam_gate: float32 [2, 1024], replicated
- new_adam_conv: float32 [2, 5, 1280], replicated
- new_adam_head: float32 [2, 3, 16], replicated
The draws below stay inside these ranges and needn't reach their ends.
Inputs may be any that keep to these rules, and one draw needn't show every extreme that they name: Each device holds 2 blocks of 128 slots, in order; a block's first block_fill slots hold tokens of one sequence and the rest are padding. A sequence fills every block but its last. Some device holds a sequence of 256 tokens, and some device has an empty block. `block_start`: 1 on every device's first block, on every block that follows a partly filled or empty one, and on empty blocks; 0 only where the block before is full and the sequence goes on. `adam_norm`: second moments are positive. `adam_gate`: second moments are positive. `adam_conv`: second moments are positive. `adam_head`: second moments are positive.
All inputs are finite; a program needn't handle non-finite values.
Results may differ from the reference program's by a relative error of at most 0.0085.
The reference program's roundings to bfloat16 on the way count: a program that leaves them out, or rounds other values in their place, can miss the bound.
Values may be sent and summed in bfloat16 or wider, within the bound.
A program may use at most 128 MiB of HBM per device.

```python
import math
import jax
import jax.numpy as jnp
from jax import lax

D = 512
H = 16
K = 4
BLOCK_LEN = 128
BLOCKS_DEV = 2
NS_STEPS = 5
ADAM_STEP = 3
E = 1024
CONV_CH = 1280
IN_COLS = 2320
TOK_DEV = 256
TOKENS = 8192
N_BLOCKS = 64


def deal_blocks(key):
    devices = N_BLOCKS // BLOCKS_DEV
    subkeys = jax.random.split(key, 4)
    pattern = jax.random.randint(subkeys[0], (devices,), 0, 3)
    pattern = pattern.at[0].set(0).at[1].set(2)
    first_len = jax.random.randint(subkeys[1], (devices,), 1, BLOCK_LEN + 1)
    second_len = jax.random.randint(subkeys[2], (devices,), 1, BLOCK_LEN + 1)
    tail_len = jax.random.randint(subkeys[3], (devices,), 1, BLOCK_LEN + 1).at[0].set(BLOCK_LEN)
    fill_first = jnp.where(pattern == 0, BLOCK_LEN, first_len)
    fill_second = jnp.where(pattern == 0, tail_len, jnp.where(pattern == 1, second_len, 0))
    start_second = jnp.where(pattern == 0, 0, 1)
    fills = jnp.stack([fill_first, fill_second], 1).reshape(-1).astype(jnp.int32)
    starts = jnp.stack([jnp.ones_like(start_second), start_second], 1).reshape(-1).astype(jnp.int32)
    return (fills, starts)


def draw_block_fill(key, part):
    return deal_blocks(jax.random.fold_in(key, 11))[0]


def draw_block_start(key, part):
    return deal_blocks(jax.random.fold_in(key, 11))[1]


def draw_head_params(key, part):
    subkeys = jax.random.split(key, 3)
    bias_row = jax.random.uniform(subkeys[0], (H,), jnp.float32, -1.0, 1.0)
    rate_row = jax.random.uniform(subkeys[1], (H,), jnp.float32, math.log(0.002), math.log(0.1))
    skip_row = jax.random.uniform(subkeys[2], (H,), jnp.float32, 0.5, 1.5)
    return jnp.stack([bias_row, rate_row, skip_row])


def adam_pair(key, shape):
    subkeys = jax.random.split(key, 2)
    first = 0.03 * jnp.clip(jax.random.normal(subkeys[0], shape, jnp.float32), -6.0, 6.0)
    second = jnp.exp(jax.random.uniform(subkeys[1], shape, jnp.float32, math.log(0.0001), math.log(0.01)))
    return jnp.stack([first, second])


def draw_adam_norm(key, part):
    return adam_pair(key, (D,))


def draw_adam_gate(key, part):
    return adam_pair(key, (E,))


def draw_adam_conv(key, part):
    return adam_pair(key, (K + 1, CONV_CH))


def draw_adam_head(key, part):
    return adam_pair(key, (3, H))


def block_levels(rng, dims, cuts, low, top_value):
    level = 1.0
    for dim, shards_of in cuts:
        draws = jax.random.uniform(jax.random.fold_in(jax.random.fold_in(rng, 6), dim), (shards_of,), jnp.float32, low / len(cuts), top_value / len(cuts))
        level = level * jnp.repeat(jnp.exp(draws), dims[dim] // shards_of).reshape((-1,) + (1,) * (len(dims) - 1 - dim))
    return level


def gaussian(rng, extent, width, bound, cuts=(), held_as=jnp.bfloat16):
    result = jax.random.normal(rng, extent, jnp.float32) * width
    if len(cuts) > 0:
        result = block_levels(rng, extent, cuts, -0.22, 0.18) * result
    return jnp.clip(result, min=-bound, max=bound).astype(held_as)


def setup_inputs(seed: int = 0) -> dict:
    seeds = jax.random.split(jax.random.key(seed), 17)
    return {
        "tokens": gaussian(seeds[0], (TOKENS, D), 1.0, 6.0, ((0, 32),)),
        "cotangent": gaussian(seeds[1], (TOKENS, D), 1.0, 6.0, ((0, 32),)),
        "block_fill": draw_block_fill(jax.random.fold_in(seeds[16], 71), 0),
        "block_start": draw_block_start(jax.random.fold_in(seeds[16], 71), 0),
        "in_weight": gaussian(seeds[4], (D, IN_COLS), D ** -0.5, 0.25, ((0, 4),), jnp.float32),
        "out_weight": gaussian(seeds[5], (E, D), E ** -0.5, 0.1875, ((0, 4),), jnp.float32),
        "in_moment": gaussian(seeds[6], (D, IN_COLS), 0.1, 1.5, ((0, 4),), jnp.float32),
        "out_moment": gaussian(seeds[7], (E, D), 0.3, 4.0, ((0, 4),), jnp.float32),
        "norm_gain": jnp.clip(1.0 + 0.1 * jax.random.normal(seeds[8], (D,), jnp.float32), 0.5, 1.5),
        "gate_gain": jnp.clip(1.0 + 0.1 * jax.random.normal(seeds[9], (E,), jnp.float32), 0.5, 1.5),
        "conv_params": jnp.clip(jax.random.uniform(seeds[10], (K + 1, CONV_CH), jnp.float32, -0.5, 0.5), -0.5, 0.5),
        "head_params": draw_head_params(jax.random.fold_in(seeds[16], 71), 0),
        "adam_norm": draw_adam_norm(jax.random.fold_in(seeds[16], 71), 0),
        "adam_gate": draw_adam_gate(jax.random.fold_in(seeds[16], 71), 0),
        "adam_conv": draw_adam_conv(jax.random.fold_in(seeds[16], 71), 0),
        "adam_head": draw_adam_head(jax.random.fold_in(seeds[16], 71), 0),
    }


highest_precision = lax.Precision.HIGHEST
norm_eps = 1e-05
schulz_coeffs = (3.4445, -4.775, 2.0315)
momentum_keep = 0.95
muon_rate = 0.05
adam_rate = 0.2
beta_first = 0.9
beta_second = 0.95
decay_rate = 0.1
adam_eps = 1e-08

def pre_norm(base, gain):
    return base * lax.rsqrt(lax.optimization_barrier(jnp.mean(base * base, -1, keepdims=True)) + norm_eps) * gain

def mixer(proj, conv_params, head_params, gate_gain, starts):
    total = proj.shape[0]
    blocks = starts.shape[0]
    length = total // blocks
    width_inner = gate_gain.shape[0]
    heads = head_params.shape[1]
    head_size = width_inner // heads
    taps = conv_params.shape[0] - 1
    channels = conv_params.shape[1]
    state_size = (channels - width_inner) // 2
    gate_in = proj[:, :width_inner]
    conv_in = proj[:, width_inner:width_inner + channels]
    dt_raw = proj[:, width_inner + channels:]
    seq_block = jnp.cumsum(starts).astype(jnp.int32)
    seq_token = jnp.repeat(seq_block, length).astype(jnp.int32)
    summed = conv_params[taps] + conv_params[taps - 1] * conv_in
    for offset in range(1, taps):
        moved = jnp.concatenate([jnp.zeros((offset, channels), jnp.float32), conv_in[:-offset]], 0)
        moved_seq = jnp.concatenate([jnp.full((offset,), -1, jnp.int32), seq_token[:-offset]], 0)
        same_seq = (moved_seq == seq_token).astype(jnp.float32)
        summed = summed + conv_params[taps - 1 - offset] * moved * same_seq[:, None]
    activated = jax.nn.silu(summed)
    values = activated[:, :width_inner].reshape(blocks, length, heads, head_size)
    b_input = activated[:, width_inner:width_inner + state_size].reshape(blocks, length, state_size)
    c_input = activated[:, width_inner + state_size:].reshape(blocks, length, state_size)
    step_size = jax.nn.softplus(dt_raw + head_params[0]).reshape(blocks, length, heads)
    rates = -jnp.exp(head_params[1])
    restart = starts.astype(jnp.float32)
    lower_mask = jnp.tril(jnp.ones((length, length), jnp.bool_))

    def advance(carry, items):
        block_vals, block_b, block_c, block_dt, fresh = items
        carry = carry * (1.0 - fresh)
        logs = jnp.cumsum(block_dt * rates, axis=0)
        columns = logs.T
        spread = columns[:, :, None] - columns[:, None, :]
        decay = jnp.where(lower_mask, jnp.exp(jnp.where(lower_mask, spread, 0.0)), 0.0)
        scores = jnp.dot(block_c, block_b.T, precision=highest_precision)
        weighted = block_vals * block_dt[:, :, None]
        local_out = jnp.einsum('hts,shp->thp', decay * scores[None], weighted, precision=highest_precision)
        carried = jnp.einsum('tn,hnp->thp', block_c, carry, precision=highest_precision) * jnp.exp(logs)[:, :, None]
        tail = jnp.exp(logs[-1][None, :] - logs)
        carry = carry * jnp.exp(logs[-1])[:, None, None] + jnp.einsum('sn,shp->hnp', block_b, weighted * tail[:, :, None], precision=highest_precision)
        return (carry, local_out + carried + head_params[2][None, :, None] * block_vals)
    initial = jnp.zeros((heads, state_size, head_size), jnp.float32)
    final_state, outputs = lax.scan(advance, initial, (values, b_input, c_input, step_size, restart))
    gated = outputs.reshape(total, width_inner) * jax.nn.silu(gate_in)
    return gated * lax.rsqrt(lax.optimization_barrier(jnp.mean(gated * gated, -1, keepdims=True)) + norm_eps) * gate_gain

def device_pass(tokens, cotangent, fill, starts, fwd_in, fwd_out, back_in, back_out, norm_gain, gate_gain, conv_params, head_params):
    total = tokens.shape[0]
    length = total // fill.shape[0]
    position = jnp.arange(total, dtype=jnp.int32) % length
    live = position < jnp.repeat(fill, length).astype(jnp.int32)
    base = tokens.astype(jnp.float32)
    normed, norm_back = jax.vjp(pre_norm, base, norm_gain)
    normed16 = normed.astype(jnp.bfloat16)
    proj = jnp.dot(normed16, fwd_in, preferred_element_type=jnp.float32)

    def mix_piece(proj_in, conv_in, head_in, gain_in):
        return mixer(proj_in, conv_in, head_in, gain_in, starts)
    mixed, mixer_back = jax.vjp(mix_piece, proj, conv_params, head_params, gate_gain)
    mixed16 = mixed.astype(jnp.bfloat16)
    branch = jnp.dot(mixed16, fwd_out, preferred_element_type=jnp.float32)
    activations = jnp.where(live[:, None], base + branch, 0.0).astype(jnp.bfloat16)
    live_cot = jnp.where(live[:, None], cotangent, jnp.zeros_like(cotangent))
    d_mixed = jnp.dot(live_cot, back_out.T, preferred_element_type=jnp.float32)
    grad_out = jnp.dot(mixed16.T, live_cot, preferred_element_type=jnp.float32)
    d_proj, grad_conv, grad_head, grad_gate = mixer_back(d_mixed)
    d_proj16 = d_proj.astype(jnp.bfloat16)
    grad_in = jnp.dot(normed16.T, d_proj16, preferred_element_type=jnp.float32)
    d_normed = jnp.dot(d_proj16, back_in.T, preferred_element_type=jnp.float32)
    d_base, grad_norm = norm_back(d_normed)
    input_grad = live_cot.astype(jnp.float32) + d_base
    return (activations, input_grad, grad_in, grad_out, grad_norm, grad_gate, grad_conv, grad_head)

def orthogonalize(matrix):
    frobenius = jnp.sqrt(jnp.sum(matrix * matrix))
    current = (matrix / (frobenius + 1e-07)).astype(jnp.bfloat16)
    flipped = matrix.shape[0] > matrix.shape[1]
    if flipped:
        current = current.T
    for turn in range(NS_STEPS):
        gram = jnp.dot(current, current.T, preferred_element_type=jnp.float32).astype(jnp.bfloat16)
        square = jnp.dot(gram, gram, preferred_element_type=jnp.float32)
        poly = (schulz_coeffs[1] * gram.astype(jnp.float32) + schulz_coeffs[2] * square).astype(jnp.bfloat16)
        current = (schulz_coeffs[0] * current.astype(jnp.float32) + jnp.dot(poly, current, preferred_element_type=jnp.float32)).astype(jnp.bfloat16)
    if flipped:
        current = current.T
    return current

def muon_apply(weight, orth, full_shape):
    factor = 0.2 * math.sqrt(max(full_shape[0], full_shape[1]))
    return weight - muon_rate * (factor * orth.astype(jnp.float32) + decay_rate * weight)

def adam_apply(param, grad, state):
    first = beta_first * state[0] + (1.0 - beta_first) * grad
    second = beta_second * state[1] + (1.0 - beta_second) * grad * grad
    first_hat = first / (1.0 - beta_first ** ADAM_STEP)
    second_hat = second / (1.0 - beta_second ** ADAM_STEP)
    updated = param - adam_rate * (first_hat / (jnp.sqrt(second_hat) + adam_eps) + decay_rate * param)
    return (updated, jnp.stack([first, second]))

def reference(tokens, cotangent, block_fill, block_start, in_weight, out_weight, in_moment, out_moment, norm_gain, gate_gain, conv_params, head_params, adam_norm, adam_gate, adam_conv, adam_head):
    devices = N_BLOCKS // BLOCKS_DEV
    in_half = in_weight.astype(jnp.bfloat16)
    out_half = out_weight.astype(jnp.bfloat16)
    tok_blocks = tokens.reshape(devices, TOK_DEV, D)
    cot_blocks = cotangent.reshape(devices, TOK_DEV, D)
    fill_blocks = block_fill.reshape(devices, BLOCKS_DEV)
    start_blocks = block_start.reshape(devices, BLOCKS_DEV)

    def one_device(carry, items):
        tok_here, cot_here, fill_here, start_here = items
        results = device_pass(tok_here, cot_here, fill_here, start_here, in_half, out_half, in_half, out_half, norm_gain, gate_gain, conv_params, head_params)
        carry = tuple((total + part for total, part in zip(carry, results[2:])))
        return (carry, (results[0], results[1]))
    zeros = (jnp.zeros((D, IN_COLS), jnp.float32), jnp.zeros((E, D), jnp.float32), jnp.zeros((D,), jnp.float32), jnp.zeros((E,), jnp.float32), jnp.zeros((K + 1, CONV_CH), jnp.float32), jnp.zeros((3, H), jnp.float32))
    sums, outputs = lax.scan(one_device, zeros, (tok_blocks, cot_blocks, fill_blocks, start_blocks))
    activations = outputs[0].reshape(TOKENS, D)
    input_grad = outputs[1].reshape(TOKENS, D)
    scale = 1.0 / math.sqrt(TOKENS)
    grad_in, grad_out, grad_norm, grad_gate, grad_conv, grad_head = [scale * part for part in sums]
    new_in_moment = momentum_keep * in_moment + grad_in
    new_out_moment = momentum_keep * out_moment + grad_out
    ranges = [(0, E), (E, 2 * E), (2 * E, IN_COLS)]
    new_pieces = []
    for lower, upper in ranges:
        orth = orthogonalize(new_in_moment[:, lower:upper])
        new_pieces.append(muon_apply(in_weight[:, lower:upper], orth, (D, upper - lower)))
    new_in_weight = jnp.concatenate(new_pieces, 1)
    new_out_weight = muon_apply(out_weight, orthogonalize(new_out_moment), (E, D))
    new_norm, state_norm = adam_apply(norm_gain, grad_norm, adam_norm)
    new_gate, state_gate = adam_apply(gate_gain, grad_gate, adam_gate)
    new_conv, state_conv = adam_apply(conv_params, grad_conv, adam_conv)
    new_head, state_head = adam_apply(head_params, grad_head, adam_head)
    return (activations, input_grad, grad_in, grad_out, grad_norm, grad_gate, grad_conv, grad_head, new_in_weight, new_out_weight, new_in_moment, new_out_moment, new_norm, new_gate, new_conv, new_head, state_norm, state_gate, state_conv, state_head)
```

```python
import math

import jax
import jax.numpy as jnp
from jax import lax
from jax.experimental import pallas as pl
from jax.experimental.pallas import tpu as pltpu
from jax.sharding import PartitionSpec as P

NS_STEPS = 5
ADAM_STEP = 3


highest_precision = lax.Precision.HIGH
norm_eps = 1e-05
schulz_coeffs = (3.4445, -4.775, 2.0315)
momentum_keep = 0.95
muon_rate = 0.05
adam_rate = 0.2
beta_first = 0.9
beta_second = 0.95
decay_rate = 0.1
adam_eps = 1e-08


def pre_norm(base, gain):
    return base * lax.rsqrt(jnp.mean(base * base, -1, keepdims=True) + norm_eps) * gain


def mixer(proj, conv_params, head_params, gate_gain, starts):
    total = proj.shape[0]
    blocks = starts.shape[0]
    length = total // blocks
    width_inner = gate_gain.shape[0]
    heads = head_params.shape[1]
    head_size = width_inner // heads
    taps = conv_params.shape[0] - 1
    channels = conv_params.shape[1]
    state_size = (channels - width_inner) // 2
    gate_in = proj[:, :width_inner]
    conv_in = proj[:, width_inner : width_inner + channels]
    dt_raw = proj[:, width_inner + channels :]
    seq_block = jnp.cumsum(starts)
    seq_token = jnp.repeat(seq_block, length)
    summed = conv_params[taps] + conv_params[taps - 1] * conv_in
    for offset in range(1, taps):
        moved = jnp.concatenate([jnp.zeros((offset, channels), jnp.float32), conv_in[:-offset]], 0)
        moved_seq = jnp.concatenate([jnp.full((offset,), -1, jnp.int32), seq_token[:-offset]], 0)
        same_seq = (moved_seq == seq_token).astype(jnp.float32)
        summed = summed + conv_params[taps - 1 - offset] * moved * same_seq[:, None]
    activated = jax.nn.silu(summed)
    values = activated[:, :width_inner].reshape(blocks, length, heads, head_size)
    b_input = activated[:, width_inner : width_inner + state_size].reshape(
        blocks, length, state_size
    )
    c_input = activated[:, width_inner + state_size :].reshape(blocks, length, state_size)
    step_size = jax.nn.softplus(dt_raw + head_params[0]).reshape(blocks, length, heads)
    rates = -jnp.exp(head_params[1])
    restart = starts.astype(jnp.float32)
    lower_mask = jnp.tril(jnp.ones((length, length), jnp.bool_))

    def advance(carry, items):
        block_vals, block_b, block_c, block_dt, fresh = items
        carry = carry * (1.0 - fresh)
        logs = jnp.cumsum(block_dt * rates, axis=0)
        columns = logs.T
        spread = columns[:, :, None] - columns[:, None, :]
        decay = jnp.where(lower_mask, jnp.exp(jnp.where(lower_mask, spread, 0.0)), 0.0)
        scores = jnp.dot(block_c, block_b.T, precision=highest_precision)
        weighted = block_vals * block_dt[:, :, None]
        local_out = jnp.einsum(
            "hts,shp->thp", decay * scores[None], weighted, precision=highest_precision
        )
        carried = (
            jnp.einsum("tn,hnp->thp", block_c, carry, precision=highest_precision)
            * jnp.exp(logs)[:, :, None]
        )
        tail = jnp.exp(logs[-1][None, :] - logs)
        carry = carry * jnp.exp(logs[-1])[:, None, None] + jnp.einsum(
            "sn,shp->hnp", block_b, weighted * tail[:, :, None], precision=highest_precision
        )
        return (carry, local_out + carried + head_params[2][None, :, None] * block_vals)

    initial = jnp.zeros((heads, state_size, head_size), jnp.float32)
    carry = initial
    pieces = []
    for block in range(blocks):
        carry, piece = advance(
            carry,
            (values[block], b_input[block], c_input[block], step_size[block], restart[block]),
        )
        pieces.append(piece)
    outputs = jnp.stack(pieces)
    gated = outputs.reshape(total, width_inner) * jax.nn.silu(gate_in)
    return gated * lax.rsqrt(jnp.mean(gated * gated, -1, keepdims=True) + norm_eps) * gate_gain


def device_pass(
    tokens,
    cotangent,
    fill,
    starts,
    fwd_in,
    fwd_out,
    back_in,
    back_out,
    norm_gain,
    gate_gain,
    conv_params,
    head_params,
):
    total = tokens.shape[0]
    length = total // fill.shape[0]
    position = jnp.arange(total, dtype=jnp.int32) % length
    live = position < jnp.repeat(fill, length)
    base = tokens.astype(jnp.float32)
    normed, norm_back = jax.vjp(pre_norm, base, norm_gain)
    normed16 = normed.astype(jnp.bfloat16)
    proj = jnp.dot(normed16, fwd_in, preferred_element_type=jnp.float32)

    def mix_piece(proj_in, conv_in, head_in, gain_in):
        return mixer(proj_in, conv_in, head_in, gain_in, starts)

    mixed, mixer_back = jax.vjp(mix_piece, proj, conv_params, head_params, gate_gain)
    mixed16 = mixed.astype(jnp.bfloat16)
    branch = jnp.dot(mixed16, fwd_out, preferred_element_type=jnp.float32)
    activations = jnp.where(live[:, None], base + branch, 0.0).astype(jnp.bfloat16)
    live_cot = jnp.where(live[:, None], cotangent, jnp.zeros_like(cotangent))
    d_mixed = jnp.dot(live_cot, back_out.T, preferred_element_type=jnp.float32)
    grad_out = jnp.dot(mixed16.T, live_cot, preferred_element_type=jnp.float32)
    d_proj, grad_conv, grad_head, grad_gate = mixer_back(d_mixed)
    d_proj16 = d_proj.astype(jnp.bfloat16)
    grad_in = jnp.dot(normed16.T, d_proj16, preferred_element_type=jnp.float32)
    d_normed = jnp.dot(d_proj16, back_in.T, preferred_element_type=jnp.float32)
    d_base, grad_norm = norm_back(d_normed)
    input_grad = live_cot.astype(jnp.float32) + d_base
    return (activations, input_grad, grad_in, grad_out, grad_norm, grad_gate, grad_conv, grad_head)


def prepare_start(matrix, pad_rows, pad_cols):
    frobenius = jnp.sqrt(jnp.sum(matrix * matrix))
    current = (matrix / (frobenius + 1e-07)).astype(jnp.bfloat16)
    if matrix.shape[0] > matrix.shape[1]:
        current = current.T
    return jnp.pad(current, ((0, pad_rows - current.shape[0]), (0, pad_cols - current.shape[1])))


def schulz_steps(current):
    for turn in range(NS_STEPS):
        gram = jnp.dot(current, current.T, preferred_element_type=jnp.float32).astype(jnp.bfloat16)
        square = jnp.dot(gram, gram, preferred_element_type=jnp.float32)
        poly = (schulz_coeffs[1] * gram.astype(jnp.float32) + schulz_coeffs[2] * square).astype(
            jnp.bfloat16
        )
        current = (
            schulz_coeffs[0] * current.astype(jnp.float32)
            + jnp.dot(poly, current, preferred_element_type=jnp.float32)
        ).astype(jnp.bfloat16)
    return current


def unpad_orth(result, shape):
    flipped = shape[0] > shape[1]
    rows_used = shape[1] if flipped else shape[0]
    cols_used = shape[0] if flipped else shape[1]
    piece = result[:rows_used, :cols_used]
    return piece.T if flipped else piece


def orth_for_device(matrices, place, shards):
    pad_rows = max((min(matrix.shape) for matrix in matrices))
    pad_cols = max((max(matrix.shape) for matrix in matrices))
    stacked = jnp.stack([prepare_start(matrix, pad_rows, pad_cols) for matrix in matrices])
    number = place * 4 // shards
    mine = lax.dynamic_index_in_dim(stacked, number, 0, keepdims=False)
    return schulz_steps(mine)


def muon_apply(weight, orth, full_shape):
    factor = 0.2 * math.sqrt(max(full_shape[0], full_shape[1]))
    return weight - muon_rate * (factor * orth.astype(jnp.float32) + decay_rate * weight)


def adam_apply(param, grad, state):
    first = beta_first * state[0] + (1.0 - beta_first) * grad
    second = beta_second * state[1] + (1.0 - beta_second) * grad * grad
    first_hat = first / (1.0 - beta_first**ADAM_STEP)
    second_hat = second / (1.0 - beta_second**ADAM_STEP)
    updated = param - adam_rate * (
        first_hat / (jnp.sqrt(second_hat) + adam_eps) + decay_rate * param
    )
    return (updated, jnp.stack([first, second]))


MESH = pl.DeviceIdType.MESH


def places():
    rep = lax.axis_index("rep")
    shard = lax.axis_index("shard")
    core = lax.rem(rep, 2)
    chip = lax.div(rep, 2)
    chips = lax.axis_size("rep") // 2
    shards = lax.axis_size("shard")
    return rep, shard, core, chip, chips, shards


def greet_peers(core, chip, shard, chips, shards):
    barrier = pltpu.get_barrier_semaphore()
    peers = [{"rep": 2 * chip + 1 - core}]
    for step in range(1, chips):
        peers.append({"rep": 2 * lax.rem(chip + step, chips) + core})
    for step in range(1, shards):
        peers.append({"shard": lax.rem(shard + step, shards)})
    for peer in peers:
        pl.semaphore_signal(barrier, inc=1, device_id=peer, device_id_type=MESH)
    pl.semaphore_wait(barrier, len(peers))


def remote(src, dst, send, recv, peer):
    return pltpu.make_async_remote_copy(
        src_ref=src, dst_ref=dst, send_sem=send, recv_sem=recv, device_id=peer, device_id_type=MESH
    )


def gather_kernel(in_ref, out_ref, all_in, all_out, own_sem, zs, zr, cs, cr, ps, pr):
    rep, shard, core, chip, chips, shards = places()
    partner = {"rep": 2 * chip + 1 - core}
    pairs = ((in_ref, all_in), (out_ref, all_out))
    own = []
    for a, (src, dst) in enumerate(pairs):
        own.append(pltpu.make_async_copy(src, dst.at[shard], own_sem.at[a]))
        own[-1].start()
    greet_peers(core, chip, shard, chips, shards)
    started = []
    for a, (src, dst) in enumerate(pairs):
        for step in range(1, shards):
            other = lax.rem(shard + step, shards)
            copy = remote(
                src.at[chip, core], dst.at[shard, chip, core],
                zs.at[a, other], zr.at[a, shard], {"shard": other},
            )
            copy.start()
            started.append(copy)
    for a, (src, dst) in enumerate(pairs):
        for step in range(1, shards):
            other = lax.rem(shard + step, shards)
            slot = dst.at[other, chip, core]
            remote(slot, slot, zs.at[a, other], zr.at[a, other], {"shard": other}).wait_recv()
            for move in range(1, chips):
                there = lax.rem(chip + move, chips)
                copy = remote(
                    slot, slot, cs.at[a, other, there], cr.at[a, other, chip],
                    {"rep": 2 * there + core},
                )
                copy.start()
                started.append(copy)
            copy = remote(slot, slot, ps.at[a, other, chip], pr.at[a, other, chip], partner)
            copy.start()
            started.append(copy)
    for a, (src, dst) in enumerate(pairs):
        for step in range(1, shards):
            other = lax.rem(shard + step, shards)
            for move in range(1, chips):
                there = lax.rem(chip + move, chips)
                slot = dst.at[other, there, core]
                remote(
                    slot, slot, cs.at[a, other, there], cr.at[a, other, there],
                    {"rep": 2 * there + core},
                ).wait_recv()
                copy = remote(slot, slot, ps.at[a, other, there], pr.at[a, other, there], partner)
                copy.start()
                started.append(copy)
    for a, (src, dst) in enumerate(pairs):
        for step in range(1, shards):
            other = lax.rem(shard + step, shards)
            for there in range(chips):
                slot = dst.at[other, there, 1 - core]
                remote(
                    slot, slot, ps.at[a, other, there], pr.at[a, other, there], partner
                ).wait_recv()
    for copy in started:
        copy.wait_send()
    for copy in own:
        copy.wait()


def gather_rows(in_half, out_half):
    chips = lax.axis_size("rep") // 2
    shards = lax.axis_size("shard")

    def split(rows):
        return rows.reshape(chips, 2, rows.shape[0] // (2 * chips), rows.shape[1])

    parts = [split(in_half), split(out_half)]
    vmem = pl.BlockSpec(memory_space=pltpu.VMEM)
    dma = pltpu.SemaphoreType.DMA
    whole = pl.pallas_call(
        gather_kernel,
        out_shape=[jax.ShapeDtypeStruct((shards,) + p.shape, p.dtype) for p in parts],
        in_specs=[vmem, vmem],
        out_specs=[vmem, vmem],
        scratch_shapes=[
            dma((2,)),
            dma((2, shards)),
            dma((2, shards)),
            dma((2, shards, chips)),
            dma((2, shards, chips)),
            dma((2, shards, chips)),
            dma((2, shards, chips)),
        ],
        compiler_params=pltpu.CompilerParams(
            collective_id=0, has_side_effects=True, vmem_limit_bytes=60 * 1024 * 1024
        ),
    )(*parts)
    return [
        w.reshape(shards * half.shape[0], half.shape[1])
        for w, half in zip(whole, (in_half, out_half))
    ]


def reduce_kernel(
    gin, gout, small, fin, fout, ftiny,
    r0i, r0o, a1i, a1o, r1i, r1o, a2i, a2o, r2i, r2o, t0, t1, t2,
    s0, v0, s1, v1, s2, v2, s3, v3, s4, v4,
):
    rep, shard, core, chip, chips, shards = places()
    partner = {"rep": 2 * chip + 1 - core}
    sources = (gin, gout)
    first = (r0i, r0o)
    sums = (a1i, a1o)
    second = (r1i, r1o)
    planes = (a2i, a2o)
    third = (r2i, r2o)
    finals = (fin, fout)
    f32 = jnp.float32
    started = []

    def go(copy):
        copy.start()
        started.append(copy)

    t0[core] = small[...]
    greet_peers(core, chip, shard, chips, shards)
    go(remote(small, t0.at[core], s0.at[2, 0], v0.at[2, 0], partner))
    order = [lax.rem(chip + move, chips) for move in range(1, chips)] + [chip]
    for there in order:
        for a in range(2):
            go(
                remote(
                    sources[a].at[:, there, 1 - core], first[a].at[there],
                    s0.at[a, there], v0.at[a, there], partner,
                )
            )
    remote(small, t0.at[1 - core], s0.at[2, 0], v0.at[2, 0], partner).wait_recv()
    t1[chip] = t0[0] + t0[1]
    for there in order[:-1]:
        peer = {"rep": 2 * there + core}
        go(remote(t1.at[chip], t1.at[chip], s1.at[2, there], v1.at[2, chip], peer))
    for number, there in enumerate(order):
        for a in range(2):
            remote(
                first[a].at[there], first[a].at[there], s0.at[a, there], v0.at[a, there], partner
            ).wait_recv()
            sums[a][there] = (
                sources[a][:, there, core].astype(f32) + first[a][there].astype(f32)
            ).astype(jnp.bfloat16)
            if number < chips - 1:
                go(
                    remote(
                        sums[a].at[there], second[a].at[chip],
                        s1.at[a, there], v1.at[a, chip], {"rep": 2 * there + core},
                    )
                )
    for there in order[:-1]:
        peer = {"rep": 2 * there + core}
        remote(t1.at[there], t1.at[there], s1.at[2, there], v1.at[2, there], peer).wait_recv()
    total = t1[0]
    for there in range(1, chips):
        total = total + t1[there]
    t2[shard] = total
    zorder = [lax.rem(shard + step, shards) for step in range(1, shards)]
    for other in zorder:
        go(remote(t2.at[shard], t2.at[shard], s2.at[2, other], v2.at[2, shard], {"shard": other}))
    for a in range(2):
        for there in order[:-1]:
            remote(
                second[a].at[there], second[a].at[there], s1.at[a, there], v1.at[a, there],
                {"rep": 2 * there + core},
            ).wait_recv()
        for other in zorder + [shard]:
            part = sums[a][chip, other].astype(f32)
            for there in order[:-1]:
                part = part + second[a][there, other].astype(f32)
            planes[a][other] = part.astype(jnp.bfloat16)
        for other in zorder:
            go(
                remote(
                    planes[a].at[other], third[a].at[shard],
                    s2.at[a, other], v2.at[a, shard], {"shard": other},
                )
            )
    for a in range(2):
        part = planes[a][shard].astype(f32)
        for other in zorder:
            remote(
                third[a].at[other], third[a].at[other], s2.at[a, other], v2.at[a, other],
                {"shard": other},
            ).wait_recv()
            part = part + third[a][other].astype(f32)
        finals[a][chip, core] = part.astype(jnp.bfloat16)
        slot = finals[a].at[chip, core]
        for there in order[:-1]:
            go(remote(slot, slot, s3.at[a, there], v3.at[a, chip], {"rep": 2 * there + core}))
        go(remote(slot, slot, s4.at[a, chip], v4.at[a, chip], partner))
    for other in zorder:
        remote(
            t2.at[other], t2.at[other], s2.at[2, other], v2.at[2, other], {"shard": other}
        ).wait_recv()
    total = t2[0]
    for other in range(1, shards):
        total = total + t2[other]
    ftiny[...] = total
    for a in range(2):
        for there in order[:-1]:
            slot = finals[a].at[there, core]
            remote(
                slot, slot, s3.at[a, there], v3.at[a, there], {"rep": 2 * there + core}
            ).wait_recv()
            go(remote(slot, slot, s4.at[a, there], v4.at[a, there], partner))
    for a in range(2):
        for there in range(chips):
            slot = finals[a].at[there, 1 - core]
            remote(slot, slot, s4.at[a, there], v4.at[a, there], partner).wait_recv()
    for copy in started:
        copy.wait_send()


def reduce_grads(grad_in, grad_out, small):
    chips = lax.axis_size("rep") // 2
    shards = lax.axis_size("shard")
    half = jnp.bfloat16

    def split(grad):
        rows = grad.shape[0] // (shards * chips * 2)
        return grad.reshape(shards, chips, 2, rows, grad.shape[1])

    parts = [split(grad_in), split(grad_out)]
    tails = [p.shape[3:] for p in parts]
    vmem = pl.BlockSpec(memory_space=pltpu.VMEM)
    dma = pltpu.SemaphoreType.DMA
    big = [pltpu.VMEM((chips, shards) + t, half) for t in tails]
    mid = [pltpu.VMEM((shards,) + t, half) for t in tails]
    fin, fout, tiny = pl.pallas_call(
        reduce_kernel,
        out_shape=[jax.ShapeDtypeStruct((chips, 2) + t, half) for t in tails]
        + [jax.ShapeDtypeStruct(small.shape, small.dtype)],
        in_specs=[vmem] * 3,
        out_specs=[vmem] * 3,
        scratch_shapes=big
        + big
        + big
        + mid
        + mid
        + [pltpu.VMEM((n,) + small.shape, small.dtype) for n in (2, chips, shards)]
        + [dma((3, chips))] * 4
        + [dma((3, shards))] * 2
        + [dma((2, chips))] * 4,
        compiler_params=pltpu.CompilerParams(
            collective_id=1, has_side_effects=True, vmem_limit_bytes=60 * 1024 * 1024
        ),
    )(*parts, small)
    return (
        fin.reshape(grad_in.shape[0] // shards, grad_in.shape[1]),
        fout.reshape(grad_out.shape[0] // shards, grad_out.shape[1]),
        tiny,
    )


def pack_small(arrays):
    flat = jnp.concatenate([a.reshape(-1) for a in arrays])
    rows = -(-flat.shape[0] // 1024) * 8
    return jnp.pad(flat, (0, rows * 128 - flat.shape[0])).reshape(rows, 128)


def unpack_small(packed, arrays):
    flat = packed.reshape(-1)
    pieces = []
    start = 0
    for a in arrays:
        pieces.append(flat[start : start + a.size].reshape(a.shape))
        start += a.size
    return pieces


def local(
    tokens,
    cotangent,
    block_fill,
    block_start,
    in_weight,
    out_weight,
    in_moment,
    out_moment,
    norm_gain,
    gate_gain,
    conv_params,
    head_params,
    adam_norm,
    adam_gate,
    adam_conv,
    adam_head,
):
    shards = lax.axis_size("shard")
    replicas = lax.axis_size("rep")
    place = lax.axis_index("shard")
    in_half = in_weight.astype(jnp.bfloat16)
    out_half = out_weight.astype(jnp.bfloat16)
    whole_in, whole_out = gather_rows(in_half, out_half)
    results = device_pass(
        tokens,
        cotangent,
        block_fill,
        block_start,
        whole_in,
        whole_out,
        whole_in,
        whole_out,
        norm_gain,
        gate_gain,
        conv_params,
        head_params,
    )
    activations, input_grad, grad_in, grad_out, grad_norm, grad_gate, grad_conv, grad_head = results
    scale = 1.0 / math.sqrt(tokens.shape[0] * shards * replicas)
    smalls = [scale * grad_norm, scale * grad_gate, scale * grad_conv, scale * grad_head]
    half_in, half_out, tiny = reduce_grads(
        (scale * grad_in).astype(jnp.bfloat16),
        (scale * grad_out).astype(jnp.bfloat16),
        pack_small(smalls),
    )
    grad_norm, grad_gate, grad_conv, grad_head = unpack_small(tiny, smalls)
    part_in = half_in.astype(jnp.float32)
    part_out = half_out.astype(jnp.float32)
    new_in_moment = momentum_keep * in_moment + part_in
    new_out_moment = momentum_keep * out_moment + part_out
    width_inner = gate_gain.shape[0]
    row_pieces = [
        new_in_moment[:, :width_inner],
        new_in_moment[:, width_inner : 2 * width_inner],
        new_in_moment[:, 2 * width_inner :],
        new_out_moment,
    ]
    full_shapes = [(piece.shape[0] * shards, piece.shape[1]) for piece in row_pieces]
    owned = []
    longest = max((piece.size for piece in row_pieces))
    outgoing = jnp.zeros((shards, longest), jnp.float32)
    for number, piece in enumerate(row_pieces):
        owner = number * shards // 4
        outgoing = outgoing.at[owner, : piece.size].set(piece.reshape(-1))
    incoming = lax.all_to_all(
        outgoing.astype(jnp.bfloat16), "shard", split_axis=0, concat_axis=0, tiled=True
    ).astype(outgoing.dtype)
    matrices = [
        incoming[:, : piece.size].reshape(full_shapes[number])
        for number, piece in enumerate(row_pieces)
    ]
    result = orth_for_device(matrices, place, shards)
    returning = jnp.zeros((shards, longest), jnp.bfloat16)
    for number, piece in enumerate(row_pieces):
        owner = number * shards // 4
        local_orth = jnp.where(
            place == owner,
            unpad_orth(result, full_shapes[number]),
            jnp.zeros(full_shapes[number], jnp.bfloat16),
        )
        returning = returning + jnp.pad(
            local_orth.reshape(shards, piece.size), ((0, 0), (0, longest - piece.size))
        )
    arrived = lax.all_to_all(returning, "shard", split_axis=0, concat_axis=0, tiled=True)
    for number, piece in enumerate(row_pieces):
        owner = number * shards // 4
        owned.append(arrived[owner, : piece.size].reshape(piece.shape))
    new_in_weight = jnp.concatenate(
        [
            muon_apply(in_weight[:, :width_inner], owned[0], full_shapes[0]),
            muon_apply(in_weight[:, width_inner : 2 * width_inner], owned[1], full_shapes[1]),
            muon_apply(in_weight[:, 2 * width_inner :], owned[2], full_shapes[2]),
        ],
        1,
    )
    new_out_weight = muon_apply(out_weight, owned[3], full_shapes[3])
    new_norm, state_norm = adam_apply(norm_gain, grad_norm, adam_norm)
    new_gate, state_gate = adam_apply(gate_gain, grad_gate, adam_gate)
    new_conv, state_conv = adam_apply(conv_params, grad_conv, adam_conv)
    new_head, state_head = adam_apply(head_params, grad_head, adam_head)
    return (
        activations,
        input_grad,
        part_in,
        part_out,
        grad_norm,
        grad_gate,
        grad_conv,
        grad_head,
        new_in_weight,
        new_out_weight,
        new_in_moment,
        new_out_moment,
        new_norm,
        new_gate,
        new_conv,
        new_head,
        state_norm,
        state_gate,
        state_conv,
        state_head,
    )


def solution(mesh):
    return jax.shard_map(
        local,
        mesh=mesh,
        in_specs=(
            P(("rep", "shard"), None),
            P(("rep", "shard"), None),
            P(("rep", "shard")),
            P(("rep", "shard")),
            P("shard", None),
            P("shard", None),
            P("shard", None),
            P("shard", None),
            P(),
            P(),
            P(),
            P(),
            P(),
            P(),
            P(),
            P(),
        ),
        out_specs=(
            P(("rep", "shard"), None),
            P(("rep", "shard"), None),
            P("shard", None),
            P("shard", None),
            P(),
            P(),
            P(),
            P(),
            P("shard", None),
            P("shard", None),
            P("shard", None),
            P("shard", None),
            P(),
            P(),
            P(),
            P(),
            P(),
            P(),
            P(),
            P(),
        ),
        check_vma=False,
    )
```

```python
import math

import jax
import jax.numpy as jnp
from jax import lax
from jax.experimental import pallas as pl
from jax.experimental.pallas import tpu as pltpu
from jax.sharding import PartitionSpec as P

NS_STEPS = 5
ADAM_STEP = 3


highest_precision = lax.Precision.HIGH
norm_eps = 1e-05
schulz_coeffs = (3.4445, -4.775, 2.0315)
momentum_keep = 0.95
muon_rate = 0.05
adam_rate = 0.2
beta_first = 0.9
beta_second = 0.95
decay_rate = 0.1
adam_eps = 1e-08


def pre_norm(base, gain):
    return base * lax.rsqrt(jnp.mean(base * base, -1, keepdims=True) + norm_eps) * gain


def mixer(proj, conv_params, head_params, gate_gain, starts):
    total = proj.shape[0]
    blocks = starts.shape[0]
    length = total // blocks
    width_inner = gate_gain.shape[0]
    heads = head_params.shape[1]
    head_size = width_inner // heads
    taps = conv_params.shape[0] - 1
    channels = conv_params.shape[1]
    state_size = (channels - width_inner) // 2
    gate_in = proj[:, :width_inner]
    conv_in = proj[:, width_inner : width_inner + channels]
    dt_raw = proj[:, width_inner + channels :]
    seq_block = jnp.cumsum(starts)
    seq_token = jnp.repeat(seq_block, length)
    summed = conv_params[taps] + conv_params[taps - 1] * conv_in
    for offset in range(1, taps):
        moved = jnp.concatenate([jnp.zeros((offset, channels), jnp.float32), conv_in[:-offset]], 0)
        moved_seq = jnp.concatenate([jnp.full((offset,), -1, jnp.int32), seq_token[:-offset]], 0)
        same_seq = (moved_seq == seq_token).astype(jnp.float32)
        summed = summed + conv_params[taps - 1 - offset] * moved * same_seq[:, None]
    activated = jax.nn.silu(summed)
    values = activated[:, :width_inner].reshape(blocks, length, heads, head_size)
    b_input = activated[:, width_inner : width_inner + state_size].reshape(
        blocks, length, state_size
    )
    c_input = activated[:, width_inner + state_size :].reshape(blocks, length, state_size)
    step_size = jax.nn.softplus(dt_raw + head_params[0]).reshape(blocks, length, heads)
    rates = -jnp.exp(head_params[1])
    restart = starts.astype(jnp.float32)
    lower_mask = jnp.tril(jnp.ones((length, length), jnp.bool_))

    def advance(carry, items):
        block_vals, block_b, block_c, block_dt, fresh = items
        carry = carry * (1.0 - fresh)
        logs = jnp.cumsum(block_dt * rates, axis=0)
        columns = logs.T
        spread = columns[:, :, None] - columns[:, None, :]
        decay = jnp.where(lower_mask, jnp.exp(jnp.where(lower_mask, spread, 0.0)), 0.0)
        scores = jnp.dot(block_c, block_b.T, precision=highest_precision)
        weighted = block_vals * block_dt[:, :, None]
        local_out = jnp.einsum(
            "hts,shp->thp", decay * scores[None], weighted, precision=highest_precision
        )
        carried = (
            jnp.einsum("tn,hnp->thp", block_c, carry, precision=highest_precision)
            * jnp.exp(logs)[:, :, None]
        )
        tail = jnp.exp(logs[-1][None, :] - logs)
        carry = carry * jnp.exp(logs[-1])[:, None, None] + jnp.einsum(
            "sn,shp->hnp", block_b, weighted * tail[:, :, None], precision=highest_precision
        )
        return (carry, local_out + carried + head_params[2][None, :, None] * block_vals)

    initial = jnp.zeros((heads, state_size, head_size), jnp.float32)
    carry = initial
    pieces = []
    for block in range(blocks):
        carry, piece = advance(
            carry,
            (values[block], b_input[block], c_input[block], step_size[block], restart[block]),
        )
        pieces.append(piece)
    outputs = jnp.stack(pieces)
    gated = outputs.reshape(total, width_inner) * jax.nn.silu(gate_in)
    return gated * lax.rsqrt(jnp.mean(gated * gated, -1, keepdims=True) + norm_eps) * gate_gain


def device_pass(
    tokens,
    cotangent,
    fill,
    starts,
    fwd_in,
    fwd_out,
    back_in,
    back_out,
    norm_gain,
    gate_gain,
    conv_params,
    head_params,
):
    total = tokens.shape[0]
    length = total // fill.shape[0]
    position = jnp.arange(total, dtype=jnp.int32) % length
    live = position < jnp.repeat(fill, length)
    base = tokens.astype(jnp.float32)
    normed, norm_back = jax.vjp(pre_norm, base, norm_gain)
    normed16 = normed.astype(jnp.bfloat16)
    proj = jnp.dot(normed16, fwd_in, preferred_element_type=jnp.float32)

    def mix_piece(proj_in, conv_in, head_in, gain_in):
        return mixer(proj_in, conv_in, head_in, gain_in, starts)

    mixed, mixer_back = jax.vjp(mix_piece, proj, conv_params, head_params, gate_gain)
    mixed16 = mixed.astype(jnp.bfloat16)
    branch = jnp.dot(mixed16, fwd_out, preferred_element_type=jnp.float32)
    activations = jnp.where(live[:, None], base + branch, 0.0).astype(jnp.bfloat16)
    live_cot = jnp.where(live[:, None], cotangent, jnp.zeros_like(cotangent))
    d_mixed = jnp.dot(live_cot, back_out.T, preferred_element_type=jnp.float32)
    grad_out = jnp.dot(mixed16.T, live_cot, preferred_element_type=jnp.float32)
    d_proj, grad_conv, grad_head, grad_gate = mixer_back(d_mixed)
    d_proj16 = d_proj.astype(jnp.bfloat16)
    grad_in = jnp.dot(normed16.T, d_proj16, preferred_element_type=jnp.float32)
    d_normed = jnp.dot(d_proj16, back_in.T, preferred_element_type=jnp.float32)
    d_base, grad_norm = norm_back(d_normed)
    input_grad = live_cot.astype(jnp.float32) + d_base
    return (activations, input_grad, grad_in, grad_out, grad_norm, grad_gate, grad_conv, grad_head)


def muon_kernel(
    mats, ret, buf, cur, gram_ref, poly_ref,
    zs, zr, cs, cr, ps, pr, zs2, zr2, cs2, cr2, ps2, pr2,
):
    rep, shard, core, chip, chips, shards = places()
    partner = {"rep": 2 * chip + 1 - core}
    count = mats.shape[0]
    rows, wide = mats.shape[3:]
    tall = shards * chips * 2 * rows
    f32 = jnp.float32
    half = jnp.bfloat16
    owners = [number * shards // count for number in range(count)]
    others = [lax.rem(shard + step, shards) for step in range(1, shards)]
    moves = [lax.rem(chip + move, chips) for move in range(1, chips)]
    greet_peers(core, chip, shard, chips, shards)

    def to_owner(number, slot):
        return remote(
            mats.at[number, chip, core], buf.at[slot, chip, core],
            zs.at[number], zr.at[slot], {"shard": owners[number]},
        )

    for number in range(count):

        @pl.when(shard != owners[number])
        def _():
            to_owner(number, shard).start()

        @pl.when(shard == owners[number])
        def _():
            buf[shard] = mats[number]

    def own_work():
        started = []
        for other in others:
            slot = buf.at[other, chip, core]
            remote(slot, slot, zs.at[0], zr.at[other], {"shard": other}).wait_recv()
            for there in moves:
                started.append(
                    remote(
                        slot, slot, cs.at[other, there], cr.at[other, chip],
                        {"rep": 2 * there + core},
                    )
                )
                started[-1].start()
            started.append(remote(slot, slot, ps.at[other, chip], pr.at[other, chip], partner))
            started[-1].start()
        for other in others:
            for there in moves:
                slot = buf.at[other, there, core]
                remote(
                    slot, slot, cs.at[other, there], cr.at[other, there],
                    {"rep": 2 * there + core},
                ).wait_recv()
                started.append(
                    remote(slot, slot, ps.at[other, there], pr.at[other, there], partner)
                )
                started[-1].start()
        for other in others:
            for there in range(chips):
                slot = buf.at[other, there, 1 - core]
                remote(
                    slot, slot, ps.at[other, there], pr.at[other, there], partner
                ).wait_recv()
        for copy in started:
            copy.wait_send()
        matrix = buf[...].reshape(tall, wide).astype(f32)
        frobenius = jnp.sqrt(jnp.sum(matrix * matrix))
        cur[...] = (matrix / (frobenius + 1e-07)).astype(half)
        left = lax.div(shard * count, shards) < 2

        def finish_poly(gram):
            gram_ref[...] = gram.astype(half)
            gram = gram_ref[...]
            square = jnp.dot(gram, gram, preferred_element_type=f32)
            poly_ref[...] = (
                schulz_coeffs[1] * gram.astype(f32) + schulz_coeffs[2] * square
            ).astype(half)

        @pl.when(left)
        def _():
            @pl.loop(0, NS_STEPS)
            def _(turn):
                now = cur[...]
                finish_poly(
                    lax.dot_general(now, now, (((1,), (1,)), ((), ())), preferred_element_type=f32)
                )
                for q in range(wide // tall):
                    part = cur[:, q * tall : (q + 1) * tall]
                    cur[:, q * tall : (q + 1) * tall] = (
                        schulz_coeffs[0] * part.astype(f32)
                        + jnp.dot(poly_ref[...], part, preferred_element_type=f32)
                    ).astype(half)

        @pl.when(jnp.logical_not(left))
        def _():
            @pl.loop(0, NS_STEPS)
            def _(turn):
                gram = jnp.zeros((tall, tall), f32)
                for q in range(wide // tall):
                    part = cur[:, q * tall : (q + 1) * tall]
                    gram = gram + lax.dot_general(
                        part, part, (((0,), (0,)), ((), ())), preferred_element_type=f32
                    )
                finish_poly(gram)
                for q in range(wide // tall):
                    part = cur[:, q * tall : (q + 1) * tall]
                    cur[:, q * tall : (q + 1) * tall] = (
                        schulz_coeffs[0] * part.astype(f32)
                        + jnp.dot(part, poly_ref[...], preferred_element_type=f32)
                    ).astype(half)

        buf[...] = cur[...].reshape(buf.shape)

    if shards <= count:
        own_work()
    else:
        pl.when(lax.rem(shard * count, shards) == 0)(own_work)

    def back(number, other):
        return remote(
            buf.at[other, chip, core], ret.at[number, chip, core],
            zs2.at[other], zr2.at[number], {"shard": other},
        )

    for number in range(count):

        @pl.when(shard == owners[number])
        def _():
            for other in others:
                back(number, other).start()
            ret[number] = buf[shard]

    def spread(number):
        slot = ret.at[number, chip, core]
        copies = [
            remote(
                slot, slot, cs2.at[number, there], cr2.at[number, chip], {"rep": 2 * there + core}
            )
            for there in moves
        ]
        return copies + [remote(slot, slot, ps2.at[number, chip], pr2.at[number, chip], partner)]

    def relay(number, there):
        slot = ret.at[number, there, core]
        return remote(slot, slot, ps2.at[number, there], pr2.at[number, there], partner)

    for number in range(count):

        @pl.when(shard != owners[number])
        def _():
            back(number, owners[number]).wait_recv()
            for copy in spread(number):
                copy.start()

    for number in range(count):

        @pl.when(shard != owners[number])
        def _():
            for there in moves:
                slot = ret.at[number, there, core]
                remote(
                    slot, slot, cs2.at[number, there], cr2.at[number, there],
                    {"rep": 2 * there + core},
                ).wait_recv()
                relay(number, there).start()

    for number in range(count):

        @pl.when(shard != owners[number])
        def _():
            for there in range(chips):
                slot = ret.at[number, there, 1 - core]
                remote(
                    slot, slot, ps2.at[number, there], pr2.at[number, there], partner
                ).wait_recv()
            to_owner(number, shard).wait_send()
            for copy in spread(number):
                copy.wait_send()
            for there in moves:
                relay(number, there).wait_send()

        @pl.when(shard == owners[number])
        def _():
            for other in others:
                back(number, other).wait_send()


def orthogonal_rows(pieces, width):
    chips = lax.axis_size("rep") // 2
    shards = lax.axis_size("shard")
    half = jnp.bfloat16
    mats = jnp.stack(pieces).astype(half)
    mats = mats.reshape(len(pieces), chips, 2, mats.shape[1] // (2 * chips), width)
    tall = shards * pieces[0].shape[0]
    vmem = pl.BlockSpec(memory_space=pltpu.VMEM)
    dma = pltpu.SemaphoreType.DMA
    count = len(pieces)
    ret = pl.pallas_call(
        muon_kernel,
        out_shape=jax.ShapeDtypeStruct(mats.shape, half),
        in_specs=[vmem],
        out_specs=vmem,
        scratch_shapes=[
            pltpu.VMEM((shards,) + mats.shape[1:], half),
            pltpu.VMEM((tall, width), half),
            pltpu.VMEM((tall, tall), half),
            pltpu.VMEM((tall, tall), half),
            dma((count,)),
            dma((shards,)),
            dma((shards, chips)),
            dma((shards, chips)),
            dma((shards, chips)),
            dma((shards, chips)),
            dma((shards,)),
            dma((count,)),
            dma((count, chips)),
            dma((count, chips)),
            dma((count, chips)),
            dma((count, chips)),
        ],
        compiler_params=pltpu.CompilerParams(
            collective_id=2, has_side_effects=True, vmem_limit_bytes=60 * 1024 * 1024
        ),
    )(mats)
    return ret.reshape(count, pieces[0].shape[0], width)


def muon_apply(weight, orth, full_shape):
    factor = 0.2 * math.sqrt(max(full_shape[0], full_shape[1]))
    return weight - muon_rate * (factor * orth.astype(jnp.float32) + decay_rate * weight)


def adam_apply(param, grad, state):
    first = beta_first * state[0] + (1.0 - beta_first) * grad
    second = beta_second * state[1] + (1.0 - beta_second) * grad * grad
    first_hat = first / (1.0 - beta_first**ADAM_STEP)
    second_hat = second / (1.0 - beta_second**ADAM_STEP)
    updated = param - adam_rate * (
        first_hat / (jnp.sqrt(second_hat) + adam_eps) + decay_rate * param
    )
    return (updated, jnp.stack([first, second]))


MESH = pl.DeviceIdType.MESH


def places():
    rep = lax.axis_index("rep")
    shard = lax.axis_index("shard")
    core = lax.rem(rep, 2)
    chip = lax.div(rep, 2)
    chips = lax.axis_size("rep") // 2
    shards = lax.axis_size("shard")
    return rep, shard, core, chip, chips, shards


def greet_peers(core, chip, shard, chips, shards):
    barrier = pltpu.get_barrier_semaphore()
    peers = [{"rep": 2 * chip + 1 - core}]
    for step in range(1, chips):
        peers.append({"rep": 2 * lax.rem(chip + step, chips) + core})
    for step in range(1, shards):
        peers.append({"shard": lax.rem(shard + step, shards)})
    for peer in peers:
        pl.semaphore_signal(barrier, inc=1, device_id=peer, device_id_type=MESH)
    pl.semaphore_wait(barrier, len(peers))


def remote(src, dst, send, recv, peer):
    return pltpu.make_async_remote_copy(
        src_ref=src, dst_ref=dst, send_sem=send, recv_sem=recv, device_id=peer, device_id_type=MESH
    )


def gather_kernel(in_ref, out_ref, all_in, all_out, own_sem, zs, zr, cs, cr, ps, pr):
    rep, shard, core, chip, chips, shards = places()
    partner = {"rep": 2 * chip + 1 - core}
    pairs = ((in_ref, all_in), (out_ref, all_out))
    own = []
    for a, (src, dst) in enumerate(pairs):
        own.append(pltpu.make_async_copy(src, dst.at[shard], own_sem.at[a]))
        own[-1].start()
    greet_peers(core, chip, shard, chips, shards)
    started = []
    for a, (src, dst) in enumerate(pairs):
        for step in range(1, shards):
            other = lax.rem(shard + step, shards)
            copy = remote(
                src.at[chip, core], dst.at[shard, chip, core],
                zs.at[a, other], zr.at[a, shard], {"shard": other},
            )
            copy.start()
            started.append(copy)
    for a, (src, dst) in enumerate(pairs):
        for step in range(1, shards):
            other = lax.rem(shard + step, shards)
            slot = dst.at[other, chip, core]
            remote(slot, slot, zs.at[a, other], zr.at[a, other], {"shard": other}).wait_recv()
            for move in range(1, chips):
                there = lax.rem(chip + move, chips)
                copy = remote(
                    slot, slot, cs.at[a, other, there], cr.at[a, other, chip],
                    {"rep": 2 * there + core},
                )
                copy.start()
                started.append(copy)
            copy = remote(slot, slot, ps.at[a, other, chip], pr.at[a, other, chip], partner)
            copy.start()
            started.append(copy)
    for a, (src, dst) in enumerate(pairs):
        for step in range(1, shards):
            other = lax.rem(shard + step, shards)
            for move in range(1, chips):
                there = lax.rem(chip + move, chips)
                slot = dst.at[other, there, core]
                remote(
                    slot, slot, cs.at[a, other, there], cr.at[a, other, there],
                    {"rep": 2 * there + core},
                ).wait_recv()
                copy = remote(slot, slot, ps.at[a, other, there], pr.at[a, other, there], partner)
                copy.start()
                started.append(copy)
    for a, (src, dst) in enumerate(pairs):
        for step in range(1, shards):
            other = lax.rem(shard + step, shards)
            for there in range(chips):
                slot = dst.at[other, there, 1 - core]
                remote(
                    slot, slot, ps.at[a, other, there], pr.at[a, other, there], partner
                ).wait_recv()
    for copy in started:
        copy.wait_send()
    for copy in own:
        copy.wait()


def gather_rows(in_half, out_half):
    chips = lax.axis_size("rep") // 2
    shards = lax.axis_size("shard")

    def split(rows):
        return rows.reshape(chips, 2, rows.shape[0] // (2 * chips), rows.shape[1])

    parts = [split(in_half), split(out_half)]
    vmem = pl.BlockSpec(memory_space=pltpu.VMEM)
    dma = pltpu.SemaphoreType.DMA
    whole = pl.pallas_call(
        gather_kernel,
        out_shape=[jax.ShapeDtypeStruct((shards,) + p.shape, p.dtype) for p in parts],
        in_specs=[vmem, vmem],
        out_specs=[vmem, vmem],
        scratch_shapes=[
            dma((2,)),
            dma((2, shards)),
            dma((2, shards)),
            dma((2, shards, chips)),
            dma((2, shards, chips)),
            dma((2, shards, chips)),
            dma((2, shards, chips)),
        ],
        compiler_params=pltpu.CompilerParams(
            collective_id=0, has_side_effects=True, vmem_limit_bytes=60 * 1024 * 1024
        ),
    )(*parts)
    return [
        w.reshape(shards * half.shape[0], half.shape[1])
        for w, half in zip(whole, (in_half, out_half))
    ]


def reduce_kernel(
    gin, gout, small, fin, fout, ftiny,
    r0i, r0o, a1i, a1o, r1i, r1o, a2i, a2o, r2i, r2o, t0, t1, t2,
    s0, v0, s1, v1, s2, v2, s3, v3, s4, v4,
):
    rep, shard, core, chip, chips, shards = places()
    partner = {"rep": 2 * chip + 1 - core}
    sources = (gin, gout)
    first = (r0i, r0o)
    sums = (a1i, a1o)
    second = (r1i, r1o)
    planes = (a2i, a2o)
    third = (r2i, r2o)
    finals = (fin, fout)
    f32 = jnp.float32
    started = []

    def go(copy):
        copy.start()
        started.append(copy)

    t0[core] = small[...]
    greet_peers(core, chip, shard, chips, shards)
    go(remote(small, t0.at[core], s0.at[2, 0], v0.at[2, 0], partner))
    order = [lax.rem(chip + move, chips) for move in range(1, chips)] + [chip]
    for there in order:
        for a in range(2):
            go(
                remote(
                    sources[a].at[:, there, 1 - core], first[a].at[there],
                    s0.at[a, there], v0.at[a, there], partner,
                )
            )
    remote(small, t0.at[1 - core], s0.at[2, 0], v0.at[2, 0], partner).wait_recv()
    t1[chip] = t0[0] + t0[1]
    for there in order[:-1]:
        peer = {"rep": 2 * there + core}
        go(remote(t1.at[chip], t1.at[chip], s1.at[2, there], v1.at[2, chip], peer))
    for number, there in enumerate(order):
        for a in range(2):
            remote(
                first[a].at[there], first[a].at[there], s0.at[a, there], v0.at[a, there], partner
            ).wait_recv()
            sums[a][there] = (
                sources[a][:, there, core].astype(f32) + first[a][there].astype(f32)
            ).astype(jnp.bfloat16)
            if number < chips - 1:
                go(
                    remote(
                        sums[a].at[there], second[a].at[chip],
                        s1.at[a, there], v1.at[a, chip], {"rep": 2 * there + core},
                    )
                )
    for there in order[:-1]:
        peer = {"rep": 2 * there + core}
        remote(t1.at[there], t1.at[there], s1.at[2, there], v1.at[2, there], peer).wait_recv()
    total = t1[0]
    for there in range(1, chips):
        total = total + t1[there]
    t2[shard] = total
    zorder = [lax.rem(shard + step, shards) for step in range(1, shards)]
    for other in zorder:
        go(remote(t2.at[shard], t2.at[shard], s2.at[2, other], v2.at[2, shard], {"shard": other}))
    for a in range(2):
        for there in order[:-1]:
            remote(
                second[a].at[there], second[a].at[there], s1.at[a, there], v1.at[a, there],
                {"rep": 2 * there + core},
            ).wait_recv()
        for other in zorder + [shard]:
            part = sums[a][chip, other].astype(f32)
            for there in order[:-1]:
                part = part + second[a][there, other].astype(f32)
            planes[a][other] = part.astype(jnp.bfloat16)
        for other in zorder:
            go(
                remote(
                    planes[a].at[other], third[a].at[shard],
                    s2.at[a, other], v2.at[a, shard], {"shard": other},
                )
            )
    for a in range(2):
        part = planes[a][shard].astype(f32)
        for other in zorder:
            remote(
                third[a].at[other], third[a].at[other], s2.at[a, other], v2.at[a, other],
                {"shard": other},
            ).wait_recv()
            part = part + third[a][other].astype(f32)
        finals[a][chip, core] = part.astype(jnp.bfloat16)
        slot = finals[a].at[chip, core]
        for there in order[:-1]:
            go(remote(slot, slot, s3.at[a, there], v3.at[a, chip], {"rep": 2 * there + core}))
        go(remote(slot, slot, s4.at[a, chip], v4.at[a, chip], partner))
    for other in zorder:
        remote(
            t2.at[other], t2.at[other], s2.at[2, other], v2.at[2, other], {"shard": other}
        ).wait_recv()
    total = t2[0]
    for other in range(1, shards):
        total = total + t2[other]
    ftiny[...] = total
    for a in range(2):
        for there in order[:-1]:
            slot = finals[a].at[there, core]
            remote(
                slot, slot, s3.at[a, there], v3.at[a, there], {"rep": 2 * there + core}
            ).wait_recv()
            go(remote(slot, slot, s4.at[a, there], v4.at[a, there], partner))
    for a in range(2):
        for there in range(chips):
            slot = finals[a].at[there, 1 - core]
            remote(slot, slot, s4.at[a, there], v4.at[a, there], partner).wait_recv()
    for copy in started:
        copy.wait_send()


def reduce_grads(grad_in, grad_out, small):
    chips = lax.axis_size("rep") // 2
    shards = lax.axis_size("shard")
    half = jnp.bfloat16

    def split(grad):
        rows = grad.shape[0] // (shards * chips * 2)
        return grad.reshape(shards, chips, 2, rows, grad.shape[1])

    parts = [split(grad_in), split(grad_out)]
    tails = [p.shape[3:] for p in parts]
    vmem = pl.BlockSpec(memory_space=pltpu.VMEM)
    dma = pltpu.SemaphoreType.DMA
    big = [pltpu.VMEM((chips, shards) + t, half) for t in tails]
    mid = [pltpu.VMEM((shards,) + t, half) for t in tails]
    fin, fout, tiny = pl.pallas_call(
        reduce_kernel,
        out_shape=[jax.ShapeDtypeStruct((chips, 2) + t, half) for t in tails]
        + [jax.ShapeDtypeStruct(small.shape, small.dtype)],
        in_specs=[vmem] * 3,
        out_specs=[vmem] * 3,
        scratch_shapes=big
        + big
        + big
        + mid
        + mid
        + [pltpu.VMEM((n,) + small.shape, small.dtype) for n in (2, chips, shards)]
        + [dma((3, chips))] * 4
        + [dma((3, shards))] * 2
        + [dma((2, chips))] * 4,
        compiler_params=pltpu.CompilerParams(
            collective_id=1, has_side_effects=True, vmem_limit_bytes=60 * 1024 * 1024
        ),
    )(*parts, small)
    return (
        fin.reshape(grad_in.shape[0] // shards, grad_in.shape[1]),
        fout.reshape(grad_out.shape[0] // shards, grad_out.shape[1]),
        tiny,
    )


def pack_small(arrays):
    flat = jnp.concatenate([a.reshape(-1) for a in arrays])
    rows = -(-flat.shape[0] // 1024) * 8
    return jnp.pad(flat, (0, rows * 128 - flat.shape[0])).reshape(rows, 128)


def unpack_small(packed, arrays):
    flat = packed.reshape(-1)
    pieces = []
    start = 0
    for a in arrays:
        pieces.append(flat[start : start + a.size].reshape(a.shape))
        start += a.size
    return pieces


def local(
    tokens,
    cotangent,
    block_fill,
    block_start,
    in_weight,
    out_weight,
    in_moment,
    out_moment,
    norm_gain,
    gate_gain,
    conv_params,
    head_params,
    adam_norm,
    adam_gate,
    adam_conv,
    adam_head,
):
    shards = lax.axis_size("shard")
    replicas = lax.axis_size("rep")
    in_half = in_weight.astype(jnp.bfloat16)
    out_half = out_weight.astype(jnp.bfloat16)
    whole_in, whole_out = gather_rows(in_half, out_half)
    results = device_pass(
        tokens,
        cotangent,
        block_fill,
        block_start,
        whole_in,
        whole_out,
        whole_in,
        whole_out,
        norm_gain,
        gate_gain,
        conv_params,
        head_params,
    )
    activations, input_grad, grad_in, grad_out, grad_norm, grad_gate, grad_conv, grad_head = results
    scale = 1.0 / math.sqrt(tokens.shape[0] * shards * replicas)
    smalls = [scale * grad_norm, scale * grad_gate, scale * grad_conv, scale * grad_head]
    half_in, half_out, tiny = reduce_grads(
        (scale * grad_in).astype(jnp.bfloat16),
        (scale * grad_out).astype(jnp.bfloat16),
        pack_small(smalls),
    )
    grad_norm, grad_gate, grad_conv, grad_head = unpack_small(tiny, smalls)
    part_in = half_in.astype(jnp.float32)
    part_out = half_out.astype(jnp.float32)
    new_in_moment = momentum_keep * in_moment + part_in
    new_out_moment = momentum_keep * out_moment + part_out
    width_inner = gate_gain.shape[0]
    rows_here = in_weight.shape[0]
    rows_all = rows_here * shards
    folds = new_out_moment.shape[0] // rows_here
    tail = in_weight.shape[1] - 2 * width_inner
    folded = jnp.transpose(
        new_out_moment.reshape(folds, rows_here, new_out_moment.shape[1]), (1, 0, 2)
    ).reshape(rows_here, width_inner)
    pieces = [
        new_in_moment[:, :width_inner],
        new_in_moment[:, width_inner : 2 * width_inner],
        jnp.pad(new_in_moment[:, 2 * width_inner :], ((0, 0), (0, width_inner - tail))),
        folded,
    ]
    orths = orthogonal_rows(pieces, width_inner)
    unfolded = jnp.transpose(
        orths[3].reshape(rows_here, folds, new_out_moment.shape[1]), (1, 0, 2)
    ).reshape(new_out_moment.shape)
    owned = [orths[0], orths[1], orths[2][:, :tail], unfolded]
    full_shapes = [
        (rows_all, width_inner),
        (rows_all, width_inner),
        (rows_all, tail),
        (new_out_moment.shape[0] * shards, new_out_moment.shape[1]),
    ]
    new_in_weight = jnp.concatenate(
        [
            muon_apply(in_weight[:, :width_inner], owned[0], full_shapes[0]),
            muon_apply(in_weight[:, width_inner : 2 * width_inner], owned[1], full_shapes[1]),
            muon_apply(in_weight[:, 2 * width_inner :], owned[2], full_shapes[2]),
        ],
        1,
    )
    new_out_weight = muon_apply(out_weight, owned[3], full_shapes[3])
    new_norm, state_norm = adam_apply(norm_gain, grad_norm, adam_norm)
    new_gate, state_gate = adam_apply(gate_gain, grad_gate, adam_gate)
    new_conv, state_conv = adam_apply(conv_params, grad_conv, adam_conv)
    new_head, state_head = adam_apply(head_params, grad_head, adam_head)
    return (
        activations,
        input_grad,
        part_in,
        part_out,
        grad_norm,
        grad_gate,
        grad_conv,
        grad_head,
        new_in_weight,
        new_out_weight,
        new_in_moment,
        new_out_moment,
        new_norm,
        new_gate,
        new_conv,
        new_head,
        state_norm,
        state_gate,
        state_conv,
        state_head,
    )


def solution(mesh):
    return jax.shard_map(
        local,
        mesh=mesh,
        in_specs=(
            P(("rep", "shard"), None),
            P(("rep", "shard"), None),
            P(("rep", "shard")),
            P(("rep", "shard")),
            P("shard", None),
            P("shard", None),
            P("shard", None),
            P("shard", None),
            P(),
            P(),
            P(),
            P(),
            P(),
            P(),
            P(),
            P(),
        ),
        out_specs=(
            P(("rep", "shard"), None),
            P(("rep", "shard"), None),
            P("shard", None),
            P("shard", None),
            P(),
            P(),
            P(),
            P(),
            P("shard", None),
            P("shard", None),
            P("shard", None),
            P("shard", None),
            P(),
            P(),
            P(),
            P(),
            P(),
            P(),
            P(),
            P(),
        ),
        check_vma=False,
    )
```

```python
import math

import jax
import jax.numpy as jnp
from jax import lax
from jax.experimental import pallas as pl
from jax.experimental.pallas import tpu as pltpu
from jax.sharding import PartitionSpec as P

NS_STEPS = 5
ADAM_STEP = 3


ssd_precision = lax.Precision.HIGH
norm_eps = 1e-05
schulz_coeffs = (3.4445, -4.775, 2.0315)
momentum_keep = 0.95
muon_rate = 0.05
adam_rate = 0.2
beta_first = 0.9
beta_second = 0.95
decay_rate = 0.1
adam_eps = 1e-08


def pre_norm(base, gain):
    return base * lax.rsqrt(jnp.mean(base * base, -1, keepdims=True) + norm_eps) * gain


def mixer(proj, conv_params, head_params, gate_gain, starts):
    total = proj.shape[0]
    blocks = starts.shape[0]
    length = total // blocks
    width_inner = gate_gain.shape[0]
    heads = head_params.shape[1]
    head_size = width_inner // heads
    taps = conv_params.shape[0] - 1
    channels = conv_params.shape[1]
    state_size = (channels - width_inner) // 2
    gate_in = proj[:, :width_inner]
    conv_in = proj[:, width_inner : width_inner + channels]
    dt_raw = proj[:, width_inner + channels :]
    seq_block = jnp.cumsum(starts)
    seq_token = jnp.repeat(seq_block, length)
    summed = conv_params[taps] + conv_params[taps - 1] * conv_in
    for offset in range(1, taps):
        moved = jnp.concatenate([jnp.zeros((offset, channels), jnp.float32), conv_in[:-offset]], 0)
        moved_seq = jnp.concatenate([jnp.full((offset,), -1, jnp.int32), seq_token[:-offset]], 0)
        same_seq = (moved_seq == seq_token).astype(jnp.float32)
        summed = summed + conv_params[taps - 1 - offset] * moved * same_seq[:, None]
    activated = jax.nn.silu(summed)
    values = activated[:, :width_inner].reshape(total, heads, head_size)
    b_input = activated[:, width_inner : width_inner + state_size]
    c_input = activated[:, width_inner + state_size :]
    step_size = jax.nn.softplus(dt_raw + head_params[0])
    rates = -jnp.exp(head_params[1])
    lower = jnp.tril(jnp.ones((total, total), jnp.bool_))
    mask = jnp.logical_and(lower, seq_token[:, None] == seq_token[None, :])
    columns = jnp.einsum(
        "ts,sh->ht", lower.astype(jnp.float32), step_size * rates, precision=lax.Precision.HIGHEST
    )
    spread = columns[:, :, None] - columns[:, None, :]
    decay = jnp.where(mask, jnp.exp(jnp.where(mask, spread, 0.0)), 0.0)
    scores = jnp.dot(c_input, b_input.T, precision=ssd_precision)
    weighted = values * step_size[:, :, None]
    outputs = jnp.einsum(
        "hts,shp->thp", decay * scores[None], weighted, precision=ssd_precision
    )
    outputs = outputs + head_params[2][None, :, None] * values
    gated = outputs.reshape(total, width_inner) * jax.nn.silu(gate_in)
    return gated * lax.rsqrt(jnp.mean(gated * gated, -1, keepdims=True) + norm_eps) * gate_gain


def device_pass(
    tokens,
    cotangent,
    fill,
    starts,
    fwd_in,
    fwd_out,
    back_in,
    back_out,
    norm_gain,
    gate_gain,
    conv_params,
    head_params,
):
    total = tokens.shape[0]
    length = total // fill.shape[0]
    position = jnp.arange(total, dtype=jnp.int32) % length
    live = position < jnp.repeat(fill, length)
    base = tokens.astype(jnp.float32)
    normed, norm_back = jax.vjp(pre_norm, base, norm_gain)
    normed16 = normed.astype(jnp.bfloat16)
    proj = jnp.dot(normed16, fwd_in, preferred_element_type=jnp.float32)

    def mix_piece(proj_in, conv_in, head_in, gain_in):
        return mixer(proj_in, conv_in, head_in, gain_in, starts)

    mixed, mixer_back = jax.vjp(mix_piece, proj, conv_params, head_params, gate_gain)
    mixed16 = mixed.astype(jnp.bfloat16)
    branch = jnp.dot(mixed16, fwd_out, preferred_element_type=jnp.float32)
    activations = jnp.where(live[:, None], base + branch, 0.0).astype(jnp.bfloat16)
    live_cot = jnp.where(live[:, None], cotangent, jnp.zeros_like(cotangent))
    d_mixed = jnp.dot(live_cot, back_out.T, preferred_element_type=jnp.float32)
    grad_out = jnp.dot(mixed16.T, live_cot, preferred_element_type=jnp.float32)
    d_proj, grad_conv, grad_head, grad_gate = mixer_back(d_mixed)
    d_proj16 = d_proj.astype(jnp.bfloat16)
    grad_in = jnp.dot(normed16.T, d_proj16, preferred_element_type=jnp.float32)
    d_normed = jnp.dot(d_proj16, back_in.T, preferred_element_type=jnp.float32)
    d_base, grad_norm = norm_back(d_normed)
    input_grad = live_cot.astype(jnp.float32) + d_base
    return (activations, input_grad, grad_in, grad_out, grad_norm, grad_gate, grad_conv, grad_head)


def muon_kernel(
    mats, ret, buf, cur, gram_ref, poly_ref,
    zs, zr, cs, cr, ps, pr, zs2, zr2, cs2, cr2, ps2, pr2,
):
    rep, shard, core, chip, chips, shards = places()
    partner = {"rep": 2 * chip + 1 - core}
    count = mats.shape[0]
    rows, wide = mats.shape[3:]
    tall = shards * chips * 2 * rows
    f32 = jnp.float32
    half = jnp.bfloat16
    owners = [number * shards // count for number in range(count)]
    others = [lax.rem(shard + step, shards) for step in range(1, shards)]
    moves = [lax.rem(chip + move, chips) for move in range(1, chips)]
    greet_peers(core, chip, shard, chips, shards)

    def to_owner(number, slot):
        return remote(
            mats.at[number, chip, core], buf.at[slot, chip, core],
            zs.at[number], zr.at[slot], {"shard": owners[number]},
        )

    for number in range(count):

        @pl.when(shard != owners[number])
        def _():
            to_owner(number, shard).start()

        @pl.when(shard == owners[number])
        def _():
            buf[shard] = mats[number]

    def own_work():
        started = []
        for other in others:
            slot = buf.at[other, chip, core]
            remote(slot, slot, zs.at[0], zr.at[other], {"shard": other}).wait_recv()
            for there in moves:
                started.append(
                    remote(
                        slot, slot, cs.at[other, there], cr.at[other, chip],
                        {"rep": 2 * there + core},
                    )
                )
                started[-1].start()
            started.append(remote(slot, slot, ps.at[other, chip], pr.at[other, chip], partner))
            started[-1].start()
        for other in others:
            for there in moves:
                slot = buf.at[other, there, core]
                remote(
                    slot, slot, cs.at[other, there], cr.at[other, there],
                    {"rep": 2 * there + core},
                ).wait_recv()
                started.append(
                    remote(slot, slot, ps.at[other, there], pr.at[other, there], partner)
                )
                started[-1].start()
        for other in others:
            for there in range(chips):
                slot = buf.at[other, there, 1 - core]
                remote(
                    slot, slot, ps.at[other, there], pr.at[other, there], partner
                ).wait_recv()
        for copy in started:
            copy.wait_send()
        matrix = buf[...].reshape(tall, wide).astype(f32)
        frobenius = jnp.sqrt(jnp.sum(matrix * matrix))
        cur[...] = (matrix / (frobenius + 1e-07)).astype(half)
        left = lax.div(shard * count, shards) < 2

        def finish_poly(gram):
            gram_ref[...] = gram.astype(half)
            gram = gram_ref[...]
            square = jnp.dot(gram, gram, preferred_element_type=f32)
            poly_ref[...] = (
                schulz_coeffs[1] * gram.astype(f32) + schulz_coeffs[2] * square
            ).astype(half)

        @pl.when(left)
        def _():
            @pl.loop(0, NS_STEPS)
            def _(turn):
                now = cur[...]
                finish_poly(
                    lax.dot_general(now, now, (((1,), (1,)), ((), ())), preferred_element_type=f32)
                )
                for q in range(wide // tall):
                    part = cur[:, q * tall : (q + 1) * tall]
                    cur[:, q * tall : (q + 1) * tall] = (
                        schulz_coeffs[0] * part.astype(f32)
                        + jnp.dot(poly_ref[...], part, preferred_element_type=f32)
                    ).astype(half)

        @pl.when(jnp.logical_not(left))
        def _():
            @pl.loop(0, NS_STEPS)
            def _(turn):
                gram = jnp.zeros((tall, tall), f32)
                for q in range(wide // tall):
                    part = cur[:, q * tall : (q + 1) * tall]
                    gram = gram + lax.dot_general(
                        part, part, (((0,), (0,)), ((), ())), preferred_element_type=f32
                    )
                finish_poly(gram)
                for q in range(wide // tall):
                    part = cur[:, q * tall : (q + 1) * tall]
                    cur[:, q * tall : (q + 1) * tall] = (
                        schulz_coeffs[0] * part.astype(f32)
                        + jnp.dot(part, poly_ref[...], preferred_element_type=f32)
                    ).astype(half)

        buf[...] = cur[...].reshape(buf.shape)

    if shards <= count:
        own_work()
    else:
        pl.when(lax.rem(shard * count, shards) == 0)(own_work)

    def back(number, other):
        return remote(
            buf.at[other, chip, core], ret.at[number, chip, core],
            zs2.at[other], zr2.at[number], {"shard": other},
        )

    for number in range(count):

        @pl.when(shard == owners[number])
        def _():
            for other in others:
                back(number, other).start()
            ret[number] = buf[shard]

    def spread(number):
        slot = ret.at[number, chip, core]
        copies = [
            remote(
                slot, slot, cs2.at[number, there], cr2.at[number, chip], {"rep": 2 * there + core}
            )
            for there in moves
        ]
        return copies + [remote(slot, slot, ps2.at[number, chip], pr2.at[number, chip], partner)]

    def relay(number, there):
        slot = ret.at[number, there, core]
        return remote(slot, slot, ps2.at[number, there], pr2.at[number, there], partner)

    for number in range(count):

        @pl.when(shard != owners[number])
        def _():
            back(number, owners[number]).wait_recv()
            for copy in spread(number):
                copy.start()

    for number in range(count):

        @pl.when(shard != owners[number])
        def _():
            for there in moves:
                slot = ret.at[number, there, core]
                remote(
                    slot, slot, cs2.at[number, there], cr2.at[number, there],
                    {"rep": 2 * there + core},
                ).wait_recv()
                relay(number, there).start()

    for number in range(count):

        @pl.when(shard != owners[number])
        def _():
            for there in range(chips):
                slot = ret.at[number, there, 1 - core]
                remote(
                    slot, slot, ps2.at[number, there], pr2.at[number, there], partner
                ).wait_recv()
            to_owner(number, shard).wait_send()
            for copy in spread(number):
                copy.wait_send()
            for there in moves:
                relay(number, there).wait_send()

        @pl.when(shard == owners[number])
        def _():
            for other in others:
                back(number, other).wait_send()


def orthogonal_rows(pieces, width):
    chips = lax.axis_size("rep") // 2
    shards = lax.axis_size("shard")
    half = jnp.bfloat16
    mats = jnp.stack(pieces).astype(half)
    mats = mats.reshape(len(pieces), chips, 2, mats.shape[1] // (2 * chips), width)
    tall = shards * pieces[0].shape[0]
    vmem = pl.BlockSpec(memory_space=pltpu.VMEM)
    dma = pltpu.SemaphoreType.DMA
    count = len(pieces)
    ret = pl.pallas_call(
        muon_kernel,
        out_shape=jax.ShapeDtypeStruct(mats.shape, half),
        in_specs=[vmem],
        out_specs=vmem,
        scratch_shapes=[
            pltpu.VMEM((shards,) + mats.shape[1:], half),
            pltpu.VMEM((tall, width), half),
            pltpu.VMEM((tall, tall), half),
            pltpu.VMEM((tall, tall), half),
            dma((count,)),
            dma((shards,)),
            dma((shards, chips)),
            dma((shards, chips)),
            dma((shards, chips)),
            dma((shards, chips)),
            dma((shards,)),
            dma((count,)),
            dma((count, chips)),
            dma((count, chips)),
            dma((count, chips)),
            dma((count, chips)),
        ],
        compiler_params=pltpu.CompilerParams(
            collective_id=2, has_side_effects=True, vmem_limit_bytes=60 * 1024 * 1024
        ),
    )(mats)
    return ret.reshape(count, pieces[0].shape[0], width)


def muon_apply(weight, orth, full_shape):
    factor = 0.2 * math.sqrt(max(full_shape[0], full_shape[1]))
    return weight - muon_rate * (factor * orth.astype(jnp.float32) + decay_rate * weight)


def adam_apply(param, grad, state):
    first = beta_first * state[0] + (1.0 - beta_first) * grad
    second = beta_second * state[1] + (1.0 - beta_second) * grad * grad
    first_hat = first / (1.0 - beta_first**ADAM_STEP)
    second_hat = second / (1.0 - beta_second**ADAM_STEP)
    updated = param - adam_rate * (
        first_hat / (jnp.sqrt(second_hat) + adam_eps) + decay_rate * param
    )
    return (updated, jnp.stack([first, second]))


MESH = pl.DeviceIdType.MESH


def places():
    rep = lax.axis_index("rep")
    shard = lax.axis_index("shard")
    core = lax.rem(rep, 2)
    chip = lax.div(rep, 2)
    chips = lax.axis_size("rep") // 2
    shards = lax.axis_size("shard")
    return rep, shard, core, chip, chips, shards


def greet_peers(core, chip, shard, chips, shards):
    barrier = pltpu.get_barrier_semaphore()
    peers = [{"rep": 2 * chip + 1 - core}]
    for step in range(1, chips):
        peers.append({"rep": 2 * lax.rem(chip + step, chips) + core})
    for step in range(1, shards):
        peers.append({"shard": lax.rem(shard + step, shards)})
    for peer in peers:
        pl.semaphore_signal(barrier, inc=1, device_id=peer, device_id_type=MESH)
    pl.semaphore_wait(barrier, len(peers))


def remote(src, dst, send, recv, peer):
    return pltpu.make_async_remote_copy(
        src_ref=src, dst_ref=dst, send_sem=send, recv_sem=recv, device_id=peer, device_id_type=MESH
    )


def gather_kernel(in_ref, out_ref, all_in, all_out, own_sem, zs, zr, cs, cr, ps, pr):
    rep, shard, core, chip, chips, shards = places()
    partner = {"rep": 2 * chip + 1 - core}
    pairs = ((in_ref, all_in), (out_ref, all_out))
    own = []
    for a, (src, dst) in enumerate(pairs):
        own.append(pltpu.make_async_copy(src, dst.at[shard], own_sem.at[a]))
        own[-1].start()
    greet_peers(core, chip, shard, chips, shards)
    started = []
    for a, (src, dst) in enumerate(pairs):
        for step in range(1, shards):
            other = lax.rem(shard + step, shards)
            copy = remote(
                src.at[chip, core], dst.at[shard, chip, core],
                zs.at[a, other], zr.at[a, shard], {"shard": other},
            )
            copy.start()
            started.append(copy)
    for a, (src, dst) in enumerate(pairs):
        for step in range(1, shards):
            other = lax.rem(shard + step, shards)
            slot = dst.at[other, chip, core]
            remote(slot, slot, zs.at[a, other], zr.at[a, other], {"shard": other}).wait_recv()
            for move in range(1, chips):
                there = lax.rem(chip + move, chips)
                copy = remote(
                    slot, slot, cs.at[a, other, there], cr.at[a, other, chip],
                    {"rep": 2 * there + core},
                )
                copy.start()
                started.append(copy)
            copy = remote(slot, slot, ps.at[a, other, chip], pr.at[a, other, chip], partner)
            copy.start()
            started.append(copy)
    for a, (src, dst) in enumerate(pairs):
        for step in range(1, shards):
            other = lax.rem(shard + step, shards)
            for move in range(1, chips):
                there = lax.rem(chip + move, chips)
                slot = dst.at[other, there, core]
                remote(
                    slot, slot, cs.at[a, other, there], cr.at[a, other, there],
                    {"rep": 2 * there + core},
                ).wait_recv()
                copy = remote(slot, slot, ps.at[a, other, there], pr.at[a, other, there], partner)
                copy.start()
                started.append(copy)
    for a, (src, dst) in enumerate(pairs):
        for step in range(1, shards):
            other = lax.rem(shard + step, shards)
            for there in range(chips):
                slot = dst.at[other, there, 1 - core]
                remote(
                    slot, slot, ps.at[a, other, there], pr.at[a, other, there], partner
                ).wait_recv()
    for copy in started:
        copy.wait_send()
    for copy in own:
        copy.wait()


def gather_rows(in_half, out_half):
    chips = lax.axis_size("rep") // 2
    shards = lax.axis_size("shard")

    def split(rows):
        return rows.reshape(chips, 2, rows.shape[0] // (2 * chips), rows.shape[1])

    parts = [split(in_half), split(out_half)]
    vmem = pl.BlockSpec(memory_space=pltpu.VMEM)
    dma = pltpu.SemaphoreType.DMA
    whole = pl.pallas_call(
        gather_kernel,
        out_shape=[jax.ShapeDtypeStruct((shards,) + p.shape, p.dtype) for p in parts],
        in_specs=[vmem, vmem],
        out_specs=[vmem, vmem],
        scratch_shapes=[
            dma((2,)),
            dma((2, shards)),
            dma((2, shards)),
            dma((2, shards, chips)),
            dma((2, shards, chips)),
            dma((2, shards, chips)),
            dma((2, shards, chips)),
        ],
        compiler_params=pltpu.CompilerParams(
            collective_id=0, has_side_effects=True, vmem_limit_bytes=60 * 1024 * 1024
        ),
    )(*parts)
    return [
        w.reshape(shards * half.shape[0], half.shape[1])
        for w, half in zip(whole, (in_half, out_half))
    ]


def reduce_kernel(
    gin, gout, small, fin, fout, ftiny,
    r0i, r0o, a1i, a1o, r1i, r1o, a2i, a2o, r2i, r2o, t0, t1, t2,
    s0, v0, s1, v1, s2, v2, s3, v3, s4, v4,
):
    rep, shard, core, chip, chips, shards = places()
    partner = {"rep": 2 * chip + 1 - core}
    sources = (gin, gout)
    first = (r0i, r0o)
    sums = (a1i, a1o)
    second = (r1i, r1o)
    planes = (a2i, a2o)
    third = (r2i, r2o)
    finals = (fin, fout)
    f32 = jnp.float32
    started = []

    def go(copy):
        copy.start()
        started.append(copy)

    t0[core] = small[...]
    greet_peers(core, chip, shard, chips, shards)
    go(remote(small, t0.at[core], s0.at[2, 0], v0.at[2, 0], partner))
    order = [lax.rem(chip + move, chips) for move in range(1, chips)] + [chip]
    for there in order:
        for a in range(2):
            go(
                remote(
                    sources[a].at[:, there, 1 - core], first[a].at[there],
                    s0.at[a, there], v0.at[a, there], partner,
                )
            )
    remote(small, t0.at[1 - core], s0.at[2, 0], v0.at[2, 0], partner).wait_recv()
    t1[chip] = t0[0] + t0[1]
    for there in order[:-1]:
        peer = {"rep": 2 * there + core}
        go(remote(t1.at[chip], t1.at[chip], s1.at[2, there], v1.at[2, chip], peer))
    for number, there in enumerate(order):
        for a in range(2):
            remote(
                first[a].at[there], first[a].at[there], s0.at[a, there], v0.at[a, there], partner
            ).wait_recv()
            sums[a][there] = (
                sources[a][:, there, core].astype(f32) + first[a][there].astype(f32)
            ).astype(jnp.bfloat16)
            if number < chips - 1:
                go(
                    remote(
                        sums[a].at[there], second[a].at[chip],
                        s1.at[a, there], v1.at[a, chip], {"rep": 2 * there + core},
                    )
                )
    for there in order[:-1]:
        peer = {"rep": 2 * there + core}
        remote(t1.at[there], t1.at[there], s1.at[2, there], v1.at[2, there], peer).wait_recv()
    total = t1[0]
    for there in range(1, chips):
        total = total + t1[there]
    t2[shard] = total
    zorder = [lax.rem(shard + step, shards) for step in range(1, shards)]
    for other in zorder:
        go(remote(t2.at[shard], t2.at[shard], s2.at[2, other], v2.at[2, shard], {"shard": other}))
    for a in range(2):
        for there in order[:-1]:
            remote(
                second[a].at[there], second[a].at[there], s1.at[a, there], v1.at[a, there],
                {"rep": 2 * there + core},
            ).wait_recv()
        for other in zorder + [shard]:
            part = sums[a][chip, other].astype(f32)
            for there in order[:-1]:
                part = part + second[a][there, other].astype(f32)
            planes[a][other] = part.astype(jnp.bfloat16)
        for other in zorder:
            go(
                remote(
                    planes[a].at[other], third[a].at[shard],
                    s2.at[a, other], v2.at[a, shard], {"shard": other},
                )
            )
    for a in range(2):
        part = planes[a][shard].astype(f32)
        for other in zorder:
            remote(
                third[a].at[other], third[a].at[other], s2.at[a, other], v2.at[a, other],
                {"shard": other},
            ).wait_recv()
            part = part + third[a][other].astype(f32)
        finals[a][chip, core] = part.astype(jnp.bfloat16)
        slot = finals[a].at[chip, core]
        for there in order[:-1]:
            go(remote(slot, slot, s3.at[a, there], v3.at[a, chip], {"rep": 2 * there + core}))
        go(remote(slot, slot, s4.at[a, chip], v4.at[a, chip], partner))
    for other in zorder:
        remote(
            t2.at[other], t2.at[other], s2.at[2, other], v2.at[2, other], {"shard": other}
        ).wait_recv()
    total = t2[0]
    for other in range(1, shards):
        total = total + t2[other]
    ftiny[...] = total
    for a in range(2):
        for there in order[:-1]:
            slot = finals[a].at[there, core]
            remote(
                slot, slot, s3.at[a, there], v3.at[a, there], {"rep": 2 * there + core}
            ).wait_recv()
            go(remote(slot, slot, s4.at[a, there], v4.at[a, there], partner))
    for a in range(2):
        for there in range(chips):
            slot = finals[a].at[there, 1 - core]
            remote(slot, slot, s4.at[a, there], v4.at[a, there], partner).wait_recv()
    for copy in started:
        copy.wait_send()


def reduce_grads(grad_in, grad_out, small):
    chips = lax.axis_size("rep") // 2
    shards = lax.axis_size("shard")
    half = jnp.bfloat16

    def split(grad):
        rows = grad.shape[0] // (shards * chips * 2)
        return grad.reshape(shards, chips, 2, rows, grad.shape[1])

    parts = [split(grad_in), split(grad_out)]
    tails = [p.shape[3:] for p in parts]
    vmem = pl.BlockSpec(memory_space=pltpu.VMEM)
    dma = pltpu.SemaphoreType.DMA
    big = [pltpu.VMEM((chips, shards) + t, half) for t in tails]
    mid = [pltpu.VMEM((shards,) + t, half) for t in tails]
    fin, fout, tiny = pl.pallas_call(
        reduce_kernel,
        out_shape=[jax.ShapeDtypeStruct((chips, 2) + t, half) for t in tails]
        + [jax.ShapeDtypeStruct(small.shape, small.dtype)],
        in_specs=[vmem] * 3,
        out_specs=[vmem] * 3,
        scratch_shapes=big
        + big
        + big
        + mid
        + mid
        + [pltpu.VMEM((n,) + small.shape, small.dtype) for n in (2, chips, shards)]
        + [dma((3, chips))] * 4
        + [dma((3, shards))] * 2
        + [dma((2, chips))] * 4,
        compiler_params=pltpu.CompilerParams(
            collective_id=1, has_side_effects=True, vmem_limit_bytes=60 * 1024 * 1024
        ),
    )(*parts, small)
    return (
        fin.reshape(grad_in.shape[0] // shards, grad_in.shape[1]),
        fout.reshape(grad_out.shape[0] // shards, grad_out.shape[1]),
        tiny,
    )


def pack_small(arrays):
    flat = jnp.concatenate([a.reshape(-1) for a in arrays])
    rows = -(-flat.shape[0] // 1024) * 8
    return jnp.pad(flat, (0, rows * 128 - flat.shape[0])).reshape(rows, 128)


def unpack_small(packed, arrays):
    flat = packed.reshape(-1)
    pieces = []
    start = 0
    for a in arrays:
        pieces.append(flat[start : start + a.size].reshape(a.shape))
        start += a.size
    return pieces


def local(
    tokens,
    cotangent,
    block_fill,
    block_start,
    in_weight,
    out_weight,
    in_moment,
    out_moment,
    norm_gain,
    gate_gain,
    conv_params,
    head_params,
    adam_norm,
    adam_gate,
    adam_conv,
    adam_head,
):
    shards = lax.axis_size("shard")
    replicas = lax.axis_size("rep")
    in_half = in_weight.astype(jnp.bfloat16)
    out_half = out_weight.astype(jnp.bfloat16)
    whole_in, whole_out = gather_rows(in_half, out_half)
    results = device_pass(
        tokens,
        cotangent,
        block_fill,
        block_start,
        whole_in,
        whole_out,
        whole_in,
        whole_out,
        norm_gain,
        gate_gain,
        conv_params,
        head_params,
    )
    activations, input_grad, grad_in, grad_out, grad_norm, grad_gate, grad_conv, grad_head = results
    scale = 1.0 / math.sqrt(tokens.shape[0] * shards * replicas)
    smalls = [scale * grad_norm, scale * grad_gate, scale * grad_conv, scale * grad_head]
    half_in, half_out, tiny = reduce_grads(
        (scale * grad_in).astype(jnp.bfloat16),
        (scale * grad_out).astype(jnp.bfloat16),
        pack_small(smalls),
    )
    grad_norm, grad_gate, grad_conv, grad_head = unpack_small(tiny, smalls)
    part_in = half_in.astype(jnp.float32)
    part_out = half_out.astype(jnp.float32)
    new_in_moment = momentum_keep * in_moment + part_in
    new_out_moment = momentum_keep * out_moment + part_out
    width_inner = gate_gain.shape[0]
    rows_here = in_weight.shape[0]
    rows_all = rows_here * shards
    folds = new_out_moment.shape[0] // rows_here
    tail = in_weight.shape[1] - 2 * width_inner
    folded = jnp.transpose(
        new_out_moment.reshape(folds, rows_here, new_out_moment.shape[1]), (1, 0, 2)
    ).reshape(rows_here, width_inner)
    pieces = [
        new_in_moment[:, :width_inner],
        new_in_moment[:, width_inner : 2 * width_inner],
        jnp.pad(new_in_moment[:, 2 * width_inner :], ((0, 0), (0, width_inner - tail))),
        folded,
    ]
    orths = orthogonal_rows(pieces, width_inner)
    unfolded = jnp.transpose(
        orths[3].reshape(rows_here, folds, new_out_moment.shape[1]), (1, 0, 2)
    ).reshape(new_out_moment.shape)
    owned = [orths[0], orths[1], orths[2][:, :tail], unfolded]
    full_shapes = [
        (rows_all, width_inner),
        (rows_all, width_inner),
        (rows_all, tail),
        (new_out_moment.shape[0] * shards, new_out_moment.shape[1]),
    ]
    new_in_weight = jnp.concatenate(
        [
            muon_apply(in_weight[:, :width_inner], owned[0], full_shapes[0]),
            muon_apply(in_weight[:, width_inner : 2 * width_inner], owned[1], full_shapes[1]),
            muon_apply(in_weight[:, 2 * width_inner :], owned[2], full_shapes[2]),
        ],
        1,
    )
    new_out_weight = muon_apply(out_weight, owned[3], full_shapes[3])
    new_norm, state_norm = adam_apply(norm_gain, grad_norm, adam_norm)
    new_gate, state_gate = adam_apply(gate_gain, grad_gate, adam_gate)
    new_conv, state_conv = adam_apply(conv_params, grad_conv, adam_conv)
    new_head, state_head = adam_apply(head_params, grad_head, adam_head)
    return (
        activations,
        input_grad,
        part_in,
        part_out,
        grad_norm,
        grad_gate,
        grad_conv,
        grad_head,
        new_in_weight,
        new_out_weight,
        new_in_moment,
        new_out_moment,
        new_norm,
        new_gate,
        new_conv,
        new_head,
        state_norm,
        state_gate,
        state_conv,
        state_head,
    )


def solution(mesh):
    return jax.shard_map(
        local,
        mesh=mesh,
        in_specs=(
            P(("rep", "shard"), None),
            P(("rep", "shard"), None),
            P(("rep", "shard")),
            P(("rep", "shard")),
            P("shard", None),
            P("shard", None),
            P("shard", None),
            P("shard", None),
            P(),
            P(),
            P(),
            P(),
            P(),
            P(),
            P(),
            P(),
        ),
        out_specs=(
            P(("rep", "shard"), None),
            P(("rep", "shard"), None),
            P("shard", None),
            P("shard", None),
            P(),
            P(),
            P(),
            P(),
            P("shard", None),
            P("shard", None),
            P("shard", None),
            P("shard", None),
            P(),
            P(),
            P(),
            P(),
            P(),
            P(),
            P(),
            P(),
        ),
        check_vma=False,
    )
```
